1024 devices in a mesh: rows: 8 (over z), cols: 8 (over x), rep: 16 (over y, core).
Axes of the slice: x: 8, y: 8, z: 8, core: 2. Of those that a mesh axis runs over, the one named last changes fastest.
Arguments:
- feature_map: bfloat16 [16, 64, 128, 384], P('rep', 'rows', 'cols'), may hold values from -6 to 6
- dw_kernel: float32 [7, 7, 384], replicated, may hold values from -0.875 to 0.875
- dw_bias: float32 [384], replicated, may hold values from -3 to 3
- layer_norm_gain: float32 [384], replicated, may hold values from 0.5 to 1.5
- layer_norm_bias: float32 [384], replicated, may hold values from -3 to 3
- w_expand: bfloat16 [384, 1536], replicated, may hold values from -0.3125 to 0.3125
- b_expand: float32 [1536], replicated, may hold values from -3 to 3
- w_reduce: bfloat16 [1536, 384], replicated, may hold values from -0.15625 to 0.15625
- b_reduce: float32 [384], replicated, may hold values from -3 to 3
- layer_scale: float32 [384], replicated, may hold values from 0.5 to 1.5
- cotangent: bfloat16 [16, 64, 128, 384], P('rep', 'rows', 'cols'), may hold values from -6 to 6
Outputs:
- block_out: bfloat16 [16, 64, 128, 384], P('rep', 'rows', 'cols')
- grad_input: bfloat16 [16, 64, 128, 384], P('rep', 'rows', 'cols')
- grad_expand: float32 [384, 1536], P('rep', ('rows', 'cols'))
- grad_reduce_t: float32 [384, 1536], P('rep', ('rows', 'cols'))
- grad_kernel: float32 [7, 7, 384], replicated
- grad_vectors: float32 [5, 384], replicated
- grad_bexp: float32 [1536], replicated
The draws below stay inside these ranges and needn't reach their ends.
All inputs are finite; a program needn't handle non-finite values.
Results may differ from the reference program's by a relative error of at most 0.0062.
Values may be sent and summed in bfloat16 or wider, within the bound.
No kernel may reach another device: no remote copies, remote signals or barrier semaphores. Data moves between devices by JAX's collectives and lax.ppermute only.
A program may use at most 32 MiB of HBM per device.

```python
import jax
import jax.numpy as jnp
from jax import lax

D = 384
FF = 1536
REGIONS = 16
H = 64
W = 128
PIXELS = 131072


def level_of(own_key, dims, split, smallest, top_value):
    def one(position, parts):
        heights = jax.random.uniform(jax.random.fold_in(jax.random.fold_in(own_key, 6), position), (parts,), jnp.float32, smallest / len(split), top_value / len(split))
        return jnp.repeat(jnp.exp(heights), dims[position] // parts).reshape((-1,) + (1,) * (len(dims) - position - 1))

    gain = one(*split[0])
    for cut in split[1:]:
        gain = gain * one(*cut)
    return gain


def gaussian(own_key, shape, scale, most, shards=(), held_as=jnp.bfloat16):
    level = level_of(own_key, shape, shards, -0.22, 0.18) if shards else 1.0
    array = jax.random.normal(own_key, shape, jnp.float32) * scale * level
    return jnp.minimum(jnp.maximum(array, -most), most).astype(held_as)


def setup_inputs(seed: int = 0) -> dict:
    streams_of = jax.random.split(jax.random.key(seed), 12)
    feature_map = gaussian(streams_of[0], (REGIONS, H, W, D), 1.0, 6.0, ((0, 16), (1, 8), (2, 8)))
    dw_kernel = gaussian(streams_of[1], (7, 7, D), 49 ** -0.5, 0.875, (), jnp.float32)
    dw_bias = gaussian(streams_of[2], (D,), 0.5, 3.0, (), jnp.float32)
    layer_norm_gain = jnp.clip(jax.random.uniform(streams_of[3], (D,), jnp.float32, 0.5, 1.5), 0.5, 1.5)
    layer_norm_bias = gaussian(streams_of[4], (D,), 0.5, 3.0, (), jnp.float32)
    w_expand = gaussian(streams_of[5], (D, FF), D ** -0.5, 0.3125)
    b_expand = gaussian(streams_of[6], (FF,), 0.5, 3.0, (), jnp.float32)
    w_reduce = gaussian(streams_of[7], (FF, D), FF ** -0.5, 0.15625)
    b_reduce = gaussian(streams_of[8], (D,), 0.5, 3.0, (), jnp.float32)
    layer_scale = jnp.clip(jax.random.uniform(streams_of[9], (D,), jnp.float32, 0.5, 1.5), 0.5, 1.5)
    cotangent = gaussian(streams_of[10], (REGIONS, H, W, D), 1.0, 6.0, ((0, 16), (1, 8), (2, 8)))
    return {"feature_map": feature_map, "dw_kernel": dw_kernel, "dw_bias": dw_bias, "layer_norm_gain": layer_norm_gain, "layer_norm_bias": layer_norm_bias, "w_expand": w_expand, "b_expand": b_expand, "w_reduce": w_reduce, "b_reduce": b_reduce, "layer_scale": layer_scale, "cotangent": cotangent}


EPS = 1e-06
INV_ROOT_TWO = 0.7071067811865476
INV_ROOT_TWO_PI = 0.3989422804014327

def depthwise(padded, kernel, height, width):
    total = jnp.zeros((height, width, padded.shape[-1]), jnp.float32)
    for i in range(7):
        for j in range(7):
            total = total + kernel[i, j] * padded[i:i + height, j:j + width].astype(jnp.float32)
    return total

def front_pass(xpad, gout, dw_kernel, dw_bias, layer_norm_gain, layer_norm_bias, w_expand, b_expand, w_reduce, b_reduce, layer_scale, height, width):
    chans = xpad.shape[-1]
    conv = depthwise(xpad, dw_kernel, height, width) + dw_bias
    flat = conv.reshape(-1, chans)
    centered_input = flat - lax.optimization_barrier(jnp.mean(flat, axis=-1, keepdims=True))
    inverse_deviation = lax.rsqrt(lax.optimization_barrier(jnp.mean(centered_input * centered_input, axis=-1, keepdims=True)) + EPS)
    standardized_input = centered_input * inverse_deviation
    normalized_rows = (standardized_input * layer_norm_gain + layer_norm_bias).astype(jnp.bfloat16)
    pre = jnp.dot(normalized_rows, w_expand, preferred_element_type=jnp.float32) + b_expand
    cdf = 0.5 * (1.0 + lax.erf(pre * INV_ROOT_TWO))
    act = (pre * cdf).astype(jnp.bfloat16)
    branch = jnp.dot(act, w_reduce, preferred_element_type=jnp.float32) + b_reduce
    inner = xpad[3:3 + height, 3:3 + width].reshape(-1, chans).astype(jnp.float32)
    block_out = (inner + layer_scale * branch).astype(jnp.bfloat16).reshape(height, width, chans)
    grad = gout.reshape(-1, chans).astype(jnp.float32)
    scaled = grad * layer_scale
    g_branch = scaled.astype(jnp.bfloat16)
    g_scale = lax.optimization_barrier(jnp.sum(grad * branch, axis=0))
    g_breduce = lax.optimization_barrier(jnp.sum(scaled, axis=0))
    grad_reduce_t = lax.dot_general(g_branch, act, (((0,), (0,)), ((), ())), preferred_element_type=jnp.float32)
    g_act = lax.dot_general(g_branch, w_reduce, (((1,), (1,)), ((), ())), preferred_element_type=jnp.float32)
    pdf = jnp.exp(-0.5 * pre * pre) * INV_ROOT_TWO_PI
    g_pre = g_act * (cdf + pre * pdf)
    g_bexp = lax.optimization_barrier(jnp.sum(g_pre, axis=0))
    g_pre_b = g_pre.astype(jnp.bfloat16)
    grad_expand = lax.dot_general(normalized_rows, g_pre_b, (((0,), (0,)), ((), ())), preferred_element_type=jnp.float32)
    grad_normalized = lax.dot_general(g_pre_b, w_expand, (((1,), (1,)), ((), ())), preferred_element_type=jnp.float32)
    grad_norm_gain = lax.optimization_barrier(jnp.sum(grad_normalized * standardized_input, axis=0))
    g_lnbias = lax.optimization_barrier(jnp.sum(grad_normalized, axis=0))
    scaled_grad_input = grad_normalized * layer_norm_gain
    grad_convolution = inverse_deviation * (scaled_grad_input - lax.optimization_barrier(jnp.mean(scaled_grad_input, axis=-1, keepdims=True)) - standardized_input * lax.optimization_barrier(jnp.mean(scaled_grad_input * standardized_input, axis=-1, keepdims=True)))
    g_dwbias = lax.optimization_barrier(jnp.sum(grad_convolution, axis=0))
    vectors = jnp.stack([g_dwbias, grad_norm_gain, g_lnbias, g_breduce, g_scale])
    return (block_out, grad_convolution.reshape(height, width, chans), grad_expand, grad_reduce_t, vectors, g_bexp)

def back_pass(gpad, xpad, gout, dw_kernel, height, width):
    inner = gpad[3:3 + height, 3:3 + width]
    grad_in = gout.astype(jnp.float32)
    kernel_rows = []
    for i in range(7):
        row_terms = []
        for j in range(7):
            part = xpad[i:i + height, j:j + width].astype(jnp.float32)
            row_terms.append(lax.optimization_barrier(jnp.sum(inner * part, axis=(0, 1))))
            grad_in = grad_in + dw_kernel[i, j] * gpad[6 - i:6 - i + height, 6 - j:6 - j + width]
        kernel_rows.append(jnp.stack(row_terms))
    return (grad_in.astype(jnp.bfloat16), jnp.stack(kernel_rows))

def reference(feature_map, dw_kernel, dw_bias, layer_norm_gain, layer_norm_bias, w_expand, b_expand, w_reduce, b_reduce, layer_scale, cotangent):
    height, width = (feature_map.shape[1], feature_map.shape[2])

    def region(pair):
        xr, gr = pair
        xpad = jnp.pad(xr, ((3, 3), (3, 3), (0, 0)))
        block_out, grad_convolution, gexp, gred, vectors, gbexp = front_pass(xpad, gr, dw_kernel, dw_bias, layer_norm_gain, layer_norm_bias, w_expand, b_expand, w_reduce, b_reduce, layer_scale, height, width)
        gpad = jnp.pad(grad_convolution, ((3, 3), (3, 3), (0, 0)))
        grad_in, gker = back_pass(gpad, xpad, gr, dw_kernel, height, width)
        return (block_out, grad_in, gexp, gred, gker, vectors, gbexp)
    outs = lax.map(region, (feature_map, cotangent))
    scale = 1.0 / jnp.sqrt(jnp.float32(PIXELS))
    return (outs[0], outs[1], lax.optimization_barrier(jnp.sum(outs[2], axis=0)) * scale, lax.optimization_barrier(jnp.sum(outs[3], axis=0)) * scale, lax.optimization_barrier(jnp.sum(outs[4], axis=0)) * scale, lax.optimization_barrier(jnp.sum(outs[5], axis=0)) * scale, lax.optimization_barrier(jnp.sum(outs[6], axis=0)) * scale)
```

```python
import functools

import jax
import jax.numpy as jnp
from jax import lax
from jax.experimental import pallas as pl
from jax.experimental.pallas import tpu as pltpu
from jax.sharding import Mesh
from jax.sharding import PartitionSpec as P

EPS = 1e-06
INV_ROOT_TWO = 0.7071067811865476
INV_ROOT_TWO_PI = 0.3989422804014327
F32 = jnp.float32
BF16 = jnp.bfloat16
D = 384
FF = 1536
LANES = 128
BLOCKS = D // LANES
HALO = 3
PIECES = 64
FROWS = FF // PIECES
DROWS = 24
BIG = BLOCKS * FROWS
ROWS = BIG + 8
LIMIT = pltpu.CompilerParams(vmem_limit_bytes=50 * 1024 * 1024)


def matmul(a, b, ca, cb):
    return lax.dot_general(a, b, (((ca,), (cb,)), ((), ())), preferred_element_type=F32)


def front_kernel(
    core_ref,
    x_ref,
    top_ref,
    bot_ref,
    left_ref,
    right_ref,
    cot_ref,
    dwk_ref,
    dwb_ref,
    gain_ref,
    lnb_ref,
    wexp_ref,
    bexp_ref,
    wred_ref,
    bred_ref,
    ls_ref,
    idx_ref,
    block_ref,
    gconv_ref,
    mine_ref,
    send_ref,
    xp,
    conv,
    both,
    small,
):
    height, width = x_ref.shape[0], x_ref.shape[1]
    pixels = height * width
    xp[HALO : HALO + height, HALO : HALO + width, :] = x_ref[...].astype(F32)
    xp[0:HALO, HALO : HALO + width, :] = top_ref[...].astype(F32)
    xp[HALO + height :, HALO : HALO + width, :] = bot_ref[...].astype(F32)
    xp[:, 0:HALO, :] = left_ref[...].astype(F32)
    xp[:, HALO + width : 2 * HALO + width, :] = right_ref[...].astype(F32)
    for l in range(BLOCKS):
        ln = slice(LANES * l, LANES * (l + 1))
        acc = jnp.zeros((height, width, LANES), F32)
        for j in range(7):
            s = xp[:, j : j + width, ln]
            for i in range(7):
                acc = acc + dwk_ref[i, j : j + 1, ln] * s[i : i + height]
        conv[:, ln] = acc.reshape(pixels, LANES)
    flat = conv[...] + dwb_ref[...]
    centered = flat - jnp.mean(flat, axis=-1, keepdims=True)
    inv = lax.rsqrt(jnp.mean(centered * centered, axis=-1, keepdims=True) + EPS)
    xhat = centered * inv
    normed = (xhat * gain_ref[...] + lnb_ref[...]).astype(BF16)
    grad = cot_ref[...].astype(F32).reshape(pixels, D)
    scaled = grad * ls_ref[...]
    g_branch = scaled.astype(BF16)
    small[...] = jnp.zeros_like(small)
    for f in range(4):
        sl = slice(D * f, D * (f + 1))
        pre = matmul(normed, wexp_ref[:, sl], 1, 0) + bexp_ref[:, sl]
        cdf = 0.5 * (1.0 + lax.erf(pre * INV_ROOT_TWO))
        pdf = jnp.exp(-0.5 * pre * pre) * INV_ROOT_TWO_PI
        g_act = matmul(g_branch, wred_ref[sl, :], 1, 1)
        g_pre = g_act * (cdf + pre * pdf)
        both[0:pixels, sl] = g_pre.astype(BF16)
        both[pixels : 2 * pixels, sl] = (pre * cdf).astype(BF16)
        row = jnp.sum(g_pre, axis=0, keepdims=True)
        for l in range(BLOCKS):
            small[54 + f, l : l + 1, :] = row[:, LANES * l : LANES * (l + 1)]
    branch = matmul(both[pixels : 2 * pixels, :], wred_ref[...], 1, 0) + bred_ref[...]
    block = x_ref[...].astype(F32).reshape(pixels, D) + ls_ref[...] * branch
    block_ref[...] = block.astype(BF16).reshape(height, width, D)
    g_norm = matmul(both[0:pixels, :], wexp_ref[...], 1, 1)
    gx = g_norm * gain_ref[...]
    gconv = inv * (
        gx
        - jnp.mean(gx, axis=-1, keepdims=True)
        - xhat * jnp.mean(gx * xhat, axis=-1, keepdims=True)
    )
    gconv_ref[...] = gconv.reshape(height, width, D)
    sums = (gconv, g_norm * xhat, g_norm, scaled, grad * branch)
    for k, value in enumerate(sums):
        row = jnp.sum(value, axis=0, keepdims=True)
        for l in range(BLOCKS):
            small[49 + k, l : l + 1, :] = row[:, LANES * l : LANES * (l + 1)]
    for l in range(BLOCKS):
        ln = slice(LANES * l, LANES * (l + 1))
        g3 = gconv_ref[:, :, ln]
        for j in range(7):
            s = xp[:, j : j + width, ln]
            for i in range(7):
                part = jnp.sum(g3 * s[i : i + height], axis=0)
                small[7 * i + j, l : l + 1, :] = jnp.sum(part, axis=0, keepdims=True)
    value = small[:, 0:BLOCKS, :]
    low = value - value.astype(BF16).astype(F32)
    mine_ref[:, BIG:ROWS, :] = small[...]
    small[:, BLOCKS : 2 * BLOCKS, :] = low
    send_ref[:, BIG:ROWS, :] = small[...].astype(BF16)
    chan = lax.broadcasted_iota(jnp.int32, (D, D), 0)
    for other in range(2):
        shift = DROWS * core_ref[0] if other == 0 else DROWS * (1 - core_ref[0])
        pick_e = (chan == idx_ref[0:1, :] + shift).astype(F32).astype(BF16)
        pick_r = (chan == idx_ref[1:2, :] + shift).astype(F32).astype(BF16)
        right = jnp.concatenate(
            [matmul(normed, pick_e, 1, 0).astype(BF16), matmul(g_branch, pick_r, 1, 0).astype(BF16)],
            axis=0,
        )
        out = mine_ref if other == 0 else send_ref
        for f in range(4):
            g = matmul(both[:, D * f : D * (f + 1)], right, 0, 0).reshape(D // FROWS, FROWS, D)
            for l in range(BLOCKS):
                out[16 * f : 16 * (f + 1), FROWS * l : FROWS * (l + 1), :] = g[
                    :, :, LANES * l : LANES * (l + 1)
                ].astype(out.dtype)


def join_kernel(mine_ref, got_ref, out_ref):
    out_ref[:, 0:BIG, :] = (mine_ref[:, 0:BIG, :] + got_ref[:, 0:BIG, :].astype(F32)).astype(BF16)
    got = got_ref[:, BIG:ROWS, :].astype(F32)
    value = mine_ref[:, BIG : BIG + BLOCKS, :] + got[:, 0:BLOCKS] + got[:, BLOCKS : 2 * BLOCKS]
    low = value - value.astype(BF16).astype(F32)
    rest = jnp.zeros((value.shape[0], 8 - 2 * BLOCKS, LANES), F32)
    out_ref[:, BIG:ROWS, :] = jnp.concatenate([value, low, rest], axis=1).astype(BF16)


def tile_sum_kernel(got_ref, out_ref):
    total = jnp.sum(got_ref[...].astype(F32), axis=0)
    wide = jnp.concatenate(
        [total[FROWS * l : FROWS * (l + 1), :] for l in range(BLOCKS)], axis=1
    )
    small = total[BIG : BIG + BLOCKS, :] + total[BIG + BLOCKS : BIG + 2 * BLOCKS, :]
    for y in range(out_ref.shape[0]):
        out_ref[y, 0:FROWS, 0 : 2 * DROWS] = wide[:, 2 * DROWS * y : 2 * DROWS * (y + 1)]
        out_ref[y, 0:FROWS, 2 * DROWS :] = jnp.zeros((FROWS, LANES - 2 * DROWS), F32)
        out_ref[y, FROWS:, :] = jnp.zeros((8, LANES), F32)
        out_ref[y, FROWS : FROWS + BLOCKS, :] = small


def region_sum_kernel(scale, got_ref, ge_ref, gr_ref, small_ref):
    total = jnp.sum(got_ref[...], axis=0) * scale
    turned = jnp.transpose(total, (1, 0))
    ge_ref[...] = turned[0:DROWS, 0:FROWS]
    gr_ref[...] = turned[DROWS : 2 * DROWS, 0:FROWS]
    small_ref[...] = jnp.broadcast_to(total[FROWS : FROWS + BLOCKS, :], small_ref.shape)


def spread_kernel(got_ref, gker_ref, vec_ref, gbexp_ref):
    for l in range(BLOCKS):
        ln = slice(LANES * l, LANES * (l + 1))
        for i in range(7):
            for j in range(7):
                gker_ref[i, j : j + 1, ln] = got_ref[7 * i + j, l : l + 1, :]
        for k in range(5):
            vec_ref[k : k + 1, ln] = got_ref[49 + k, l : l + 1, :]
        for f in range(4):
            at = D * f + LANES * l
            gbexp_ref[0:1, at : at + LANES] = got_ref[54 + f, l : l + 1, :]


def input_grad_kernel(g_ref, top_ref, bot_ref, left_ref, right_ref, cot_ref, dwk_ref, out_ref, gp):
    height, width = g_ref.shape[0], g_ref.shape[1]
    gp[HALO : HALO + height, HALO : HALO + width, :] = g_ref[...]
    gp[0:HALO, HALO : HALO + width, :] = top_ref[...]
    gp[HALO + height :, HALO : HALO + width, :] = bot_ref[...]
    gp[:, 0:HALO, :] = left_ref[...]
    gp[:, HALO + width : 2 * HALO + width, :] = right_ref[...]
    for l in range(BLOCKS):
        ln = slice(LANES * l, LANES * (l + 1))
        acc = cot_ref[:, :, ln].astype(F32)
        for j in range(7):
            s = gp[:, 6 - j : 6 - j + width, ln]
            for i in range(7):
                acc = acc + dwk_ref[i, j : j + 1, ln] * s[6 - i : 6 - i + height]
        out_ref[:, :, ln] = acc.astype(BF16)


def shifted(cells, axis, dim):
    count = lax.axis_size(axis)
    size = cells.shape[dim]
    head = lax.slice_in_dim(cells, 0, HALO, axis=dim)
    tail = lax.slice_in_dim(cells, size - HALO, size, axis=dim)
    before = lax.ppermute(tail, axis, [(i, i + 1) for i in range(count - 1)])
    after = lax.ppermute(head, axis, [(i + 1, i) for i in range(count - 1)])
    return before, after


def column_halo(cells, top, bot):
    width = cells.shape[1]
    head = jnp.concatenate([a[:, 0:HALO] for a in (top, cells, bot)], axis=0)
    tail = jnp.concatenate([a[:, width - HALO :] for a in (top, cells, bot)], axis=0)
    count = lax.axis_size("cols")
    left = lax.ppermute(tail, "cols", [(i, i + 1) for i in range(count - 1)])
    right = lax.ppermute(head, "cols", [(i + 1, i) for i in range(count - 1)])
    return left, right


def per_device(
    scale,
    feature_map,
    dw_kernel,
    dw_bias,
    layer_norm_gain,
    layer_norm_bias,
    w_expand,
    b_expand,
    w_reduce,
    b_reduce,
    layer_scale,
    cotangent,
):
    x, cot = feature_map[0], cotangent[0]
    height, width = x.shape[0], x.shape[1]
    regions = lax.axis_size("y")
    core = lax.axis_index("core").astype(jnp.int32)
    top, bot = shifted(x, "rows", 0)
    left, right = column_halo(x, top, bot)

    column = jnp.arange(D, dtype=jnp.int32)
    block, kind, inside = column // (2 * DROWS), (column // DROWS) % 2, column % DROWS
    base = 2 * DROWS * block + inside
    away = jnp.int32(-4 * D)
    index = jnp.stack([jnp.where(kind == 0, base, away), jnp.where(kind == 1, base, away)])

    row = lambda v: v.reshape(1, -1)
    whole = lambda n: [pl.BlockSpec(memory_space=pltpu.VMEM)] * n
    block_out, gconv, mine, send = pl.pallas_call(
        front_kernel,
        out_shape=(
            jax.ShapeDtypeStruct((height, width, D), BF16),
            jax.ShapeDtypeStruct((height, width, D), F32),
            jax.ShapeDtypeStruct((PIECES, ROWS, LANES), F32),
            jax.ShapeDtypeStruct((PIECES, ROWS, LANES), BF16),
        ),
        in_specs=[pl.BlockSpec(memory_space=pltpu.SMEM)] + whole(16),
        out_specs=tuple(whole(4)),
        scratch_shapes=[
            pltpu.VMEM((height + 2 * HALO, width + 8, D), F32),
            pltpu.VMEM((height * width, D), F32),
            pltpu.VMEM((2 * height * width, FF), BF16),
            pltpu.VMEM((PIECES, 8, LANES), F32),
        ],
        compiler_params=LIMIT,
        name="front",
    )(
        core.reshape(1),
        x,
        top,
        bot,
        left,
        right,
        cot,
        dw_kernel,
        row(dw_bias),
        row(layer_norm_gain),
        row(layer_norm_bias),
        w_expand,
        row(b_expand),
        w_reduce,
        row(b_reduce),
        row(layer_scale),
        index,
    )

    got = lax.ppermute(send, "core", [(0, 1), (1, 0)])
    gtop, gbot = shifted(gconv, "rows", 0)
    gleft, gright = column_halo(gconv, gtop, gbot)

    step = 16
    spec = pl.BlockSpec((step, ROWS, LANES), lambda i: (i, 0, 0))
    joined = pl.pallas_call(
        join_kernel,
        out_shape=jax.ShapeDtypeStruct((PIECES, ROWS, LANES), BF16),
        grid=(PIECES // step,),
        in_specs=[spec, spec],
        out_specs=spec,
        compiler_params=LIMIT,
        name="join",
    )(mine, got)
    tiles = lax.all_to_all(joined, ("rows", "cols"), 0, 0, tiled=True)
    by_region = pl.pallas_call(
        tile_sum_kernel,
        out_shape=jax.ShapeDtypeStruct((regions, FROWS + 8, LANES), F32),
        in_specs=whole(1),
        out_specs=whole(1)[0],
        compiler_params=LIMIT,
        name="tile_sum",
    )(tiles)
    by_region = lax.all_to_all(by_region, "y", 0, 0, tiled=True)
    grad_expand, grad_reduce_t, small = pl.pallas_call(
        functools.partial(region_sum_kernel, scale),
        out_shape=(
            jax.ShapeDtypeStruct((DROWS, FROWS), F32),
            jax.ShapeDtypeStruct((DROWS, FROWS), F32),
            jax.ShapeDtypeStruct((PIECES, BLOCKS, LANES), F32),
        ),
        in_specs=whole(1),
        out_specs=tuple(whole(3)),
        compiler_params=LIMIT,
        name="region_sum",
    )(by_region)
    small = lax.all_to_all(small, ("rows", "cols"), 0, 0, tiled=True)
    gker, vectors, gbexp = pl.pallas_call(
        spread_kernel,
        out_shape=(
            jax.ShapeDtypeStruct((7, 7, D), F32),
            jax.ShapeDtypeStruct((5, D), F32),
            jax.ShapeDtypeStruct((1, FF), F32),
        ),
        in_specs=whole(1),
        out_specs=tuple(whole(3)),
        compiler_params=LIMIT,
        name="spread",
    )(small)
    grad_in = pl.pallas_call(
        input_grad_kernel,
        out_shape=jax.ShapeDtypeStruct((height, width, D), BF16),
        in_specs=whole(7),
        out_specs=whole(1)[0],
        scratch_shapes=[pltpu.VMEM((height + 2 * HALO, width + 8, D), F32)],
        compiler_params=LIMIT,
        name="input_grad",
    )(gconv, gtop, gbot, gleft, gright, cot, dw_kernel)
    return (
        block_out[None],
        grad_in[None],
        grad_expand,
        grad_reduce_t,
        gker,
        vectors,
        gbexp.reshape(FF),
    )


def solution(mesh):
    shape = dict(mesh.shape)
    fine = Mesh(
        mesh.devices.reshape(shape["rows"], shape["cols"], shape["rep"] // 2, 2),
        ("rows", "cols", "y", "core"),
    )
    tile = P(("y", "core"), "rows", "cols", None)
    grad = P(("y", "core"), ("rows", "cols"))
    pixels = 16 * 64 * 128
    scale = float(pixels) ** -0.5
    return jax.shard_map(
        functools.partial(per_device, scale),
        mesh=fine,
        in_specs=(tile,) + (P(),) * 9 + (tile,),
        out_specs=(tile, tile, grad, grad, P(), P(), P()),
        check_vma=False,
    )
```

```python
import functools

import jax
import jax.numpy as jnp
from jax import lax
from jax.experimental import pallas as pl
from jax.experimental.pallas import tpu as pltpu
from jax.sharding import Mesh
from jax.sharding import PartitionSpec as P

EPS = 1e-06
INV_ROOT_TWO = 0.7071067811865476
INV_ROOT_TWO_PI = 0.3989422804014327
F32 = jnp.float32
BF16 = jnp.bfloat16
D = 384
FF = 1536
LANES = 128
BLOCKS = D // LANES
HALO = 3
PIECES = 64
FROWS = FF // PIECES
DROWS = 24
BIG = BLOCKS * FROWS
ROWS = BIG + 8
LIMIT = pltpu.CompilerParams(vmem_limit_bytes=50 * 1024 * 1024)


def matmul(a, b, ca, cb):
    return lax.dot_general(a, b, (((ca,), (cb,)), ((), ())), preferred_element_type=F32)


def front_kernel(
    core_ref,
    x_hbm,
    top_ref,
    bot_ref,
    left_ref,
    right_ref,
    cot_hbm,
    dwk_hbm,
    dwb_hbm,
    gain_hbm,
    lnb_hbm,
    wexp_hbm,
    bexp_hbm,
    wred_hbm,
    bred_hbm,
    ls_hbm,
    block_ref,
    gconv_ref,
    mine_hbm,
    send_hbm,
    x_ref,
    cot_ref,
    dwk_ref,
    dwb_ref,
    gain_ref,
    lnb_ref,
    wexp_ref,
    bexp_ref,
    wred_ref,
    bred_ref,
    ls_ref,
    xp,
    conv,
    both,
    small,
    mine_ref,
    send_ref,
    sems,
):
    pairs = (
        (x_hbm, x_ref),
        (dwk_hbm, dwk_ref),
        (dwb_hbm, dwb_ref),
        (gain_hbm, gain_ref),
        (lnb_hbm, lnb_ref),
        (cot_hbm, cot_ref),
        (ls_hbm, ls_ref),
        (bexp_hbm, bexp_ref),
        (bred_hbm, bred_ref),
        (wexp_hbm, wexp_ref),
        (wred_hbm, wred_ref),
    )
    copies = [pltpu.make_async_copy(a, b, sems.at[k]) for k, (a, b) in enumerate(pairs)]
    for c in copies:
        c.start()
    height, width = x_ref.shape[0], x_ref.shape[1]
    pixels = height * width
    row = lambda ref: ref[...].reshape(1, -1)
    xp[0:HALO, HALO : HALO + width, :] = top_ref[...].astype(F32)
    xp[HALO + height :, HALO : HALO + width, :] = bot_ref[...].astype(F32)
    xp[:, 0:HALO, :] = left_ref[...].astype(F32)
    xp[:, HALO + width : 2 * HALO + width, :] = right_ref[...].astype(F32)
    small[...] = jnp.zeros_like(small)
    for c in copies[0:2]:
        c.wait()
    xp[HALO : HALO + height, HALO : HALO + width, :] = x_ref[...].astype(F32)
    for l in range(BLOCKS):
        ln = slice(LANES * l, LANES * (l + 1))
        acc = jnp.zeros((height, width, LANES), F32)
        for j in range(7):
            s = xp[:, j : j + width, ln]
            for i in range(7):
                acc = acc + dwk_ref[i, j : j + 1, ln] * s[i : i + height]
        conv[:, ln] = acc.reshape(pixels, LANES)
    for c in copies[2:]:
        c.wait()
    flat = conv[...] + row(dwb_ref)
    centered = flat - jnp.mean(flat, axis=-1, keepdims=True)
    inv = lax.rsqrt(jnp.mean(centered * centered, axis=-1, keepdims=True) + EPS)
    xhat = centered * inv
    gain = row(gain_ref)
    normed = (xhat * gain + row(lnb_ref)).astype(BF16)
    grad = cot_ref[...].astype(F32).reshape(pixels, D)
    scaled = grad * row(ls_ref)
    g_branch = scaled.astype(BF16)
    for f in range(4):
        sl = slice(D * f, D * (f + 1))
        pre = matmul(normed, wexp_ref[:, sl], 1, 0) + bexp_ref[sl].reshape(1, D)
        cdf = 0.5 * (1.0 + lax.erf(pre * INV_ROOT_TWO))
        pdf = jnp.exp(-0.5 * pre * pre) * INV_ROOT_TWO_PI
        g_act = matmul(g_branch, wred_ref[sl, :], 1, 1)
        g_pre = g_act * (cdf + pre * pdf)
        both[0:pixels, sl] = g_pre.astype(BF16)
        both[pixels : 2 * pixels, sl] = (pre * cdf).astype(BF16)
        total = jnp.sum(g_pre, axis=0, keepdims=True)
        for l in range(BLOCKS):
            small[54 + f, l : l + 1, :] = total[:, LANES * l : LANES * (l + 1)]
    branch = matmul(both[pixels : 2 * pixels, :], wred_ref[...], 1, 0) + row(bred_ref)
    block = x_ref[...].astype(F32).reshape(pixels, D) + row(ls_ref) * branch
    block_ref[...] = block.astype(BF16).reshape(height, width, D)
    g_norm = matmul(both[0:pixels, :], wexp_ref[...], 1, 1)
    gx = g_norm * gain
    gconv = inv * (
        gx
        - jnp.mean(gx, axis=-1, keepdims=True)
        - xhat * jnp.mean(gx * xhat, axis=-1, keepdims=True)
    )
    gconv_ref[...] = gconv.reshape(height, width, D)
    sums = (gconv, g_norm * xhat, g_norm, scaled, grad * branch)
    for k, value in enumerate(sums):
        total = jnp.sum(value, axis=0, keepdims=True)
        for l in range(BLOCKS):
            small[49 + k, l : l + 1, :] = total[:, LANES * l : LANES * (l + 1)]
    for l in range(BLOCKS):
        ln = slice(LANES * l, LANES * (l + 1))
        g3 = gconv_ref[:, :, ln]
        for j in range(7):
            s = xp[:, j : j + width, ln]
            for i in range(7):
                part = jnp.sum(g3 * s[i : i + height], axis=0)
                small[7 * i + j, l : l + 1, :] = jnp.sum(part, axis=0, keepdims=True)
    value = small[:, 0:BLOCKS, :]
    small[:, BLOCKS : 2 * BLOCKS, :] = value - value.astype(BF16).astype(F32)
    packed = small[...].astype(BF16)
    chan = lax.broadcasted_iota(jnp.int32, (D, D), 0)
    column = lax.broadcasted_iota(jnp.int32, (1, D), 1)
    block = (column * 1366) >> 16
    inside = column - 2 * DROWS * block
    of_e = 2 * DROWS * block + jnp.where(inside < DROWS, inside, -4 * D)
    of_r = 2 * DROWS * block + jnp.where(inside < DROWS, -4 * D, inside - DROWS)
    outputs = []
    for which, (out, hbm) in enumerate(((send_ref, send_hbm), (mine_ref, mine_hbm))):
        shift = DROWS * core_ref[0] if which == 1 else DROWS * (1 - core_ref[0])
        out[:, BIG:ROWS, :] = packed
        pick_e = (chan == of_e + shift).astype(F32).astype(BF16)
        pick_r = (chan == of_r + shift).astype(F32).astype(BF16)
        right = jnp.concatenate(
            [matmul(normed, pick_e, 1, 0).astype(BF16), matmul(g_branch, pick_r, 1, 0).astype(BF16)],
            axis=0,
        )
        for f in range(4):
            g = matmul(both[:, D * f : D * (f + 1)], right, 0, 0).reshape(D // FROWS, FROWS, D)
            at = slice(16 * f, 16 * (f + 1))
            for l in range(BLOCKS):
                out[at, FROWS * l : FROWS * (l + 1), :] = g[
                    :, :, LANES * l : LANES * (l + 1)
                ].astype(BF16)
            c = pltpu.make_async_copy(out.at[at], hbm.at[at], sems.at[11 + 4 * which + f])
            c.start()
            outputs.append(c)
    for c in outputs:
        c.wait()


def join_kernel(mine_ref, got_ref, out_ref):
    big = mine_ref[:, 0:BIG, :].astype(F32) + got_ref[:, 0:BIG, :].astype(F32)
    out_ref[:, 0:BIG, :] = big.astype(BF16)
    both = mine_ref[:, BIG:ROWS, :].astype(F32) + got_ref[:, BIG:ROWS, :].astype(F32)
    value = both[:, 0:BLOCKS] + both[:, BLOCKS : 2 * BLOCKS]
    low = value - value.astype(BF16).astype(F32)
    rest = jnp.zeros((value.shape[0], 8 - 2 * BLOCKS, LANES), F32)
    out_ref[:, BIG:ROWS, :] = jnp.concatenate([value, low, rest], axis=1).astype(BF16)


def tile_sum_kernel(got_ref, after_hbm, out_ref):
    total = jnp.sum(got_ref[...].astype(F32), axis=0)
    wide = jnp.concatenate(
        [total[FROWS * l : FROWS * (l + 1), :] for l in range(BLOCKS)], axis=1
    )
    small = total[BIG : BIG + BLOCKS, :] + total[BIG + BLOCKS : BIG + 2 * BLOCKS, :]
    for y in range(out_ref.shape[0]):
        out_ref[y, 0:FROWS, 0 : 2 * DROWS] = wide[:, 2 * DROWS * y : 2 * DROWS * (y + 1)]
        out_ref[y, 0:FROWS, 2 * DROWS :] = jnp.zeros((FROWS, LANES - 2 * DROWS), F32)
        out_ref[y, FROWS:, :] = jnp.zeros((8, LANES), F32)
        out_ref[y, FROWS : FROWS + BLOCKS, :] = small


def region_sum_kernel(scale, got_ref, ge_ref, gr_ref, small_ref):
    total = jnp.sum(got_ref[...], axis=0) * scale
    turned = jnp.transpose(total, (1, 0))
    ge_ref[...] = turned[0:DROWS, 0:FROWS]
    gr_ref[...] = turned[DROWS : 2 * DROWS, 0:FROWS]
    small_ref[...] = jnp.broadcast_to(total[FROWS : FROWS + BLOCKS, :], small_ref.shape)


def spread_kernel(got_ref, gker_ref, vec_ref, gbexp_ref):
    for l in range(BLOCKS):
        ln = slice(LANES * l, LANES * (l + 1))
        for i in range(7):
            for j in range(7):
                gker_ref[i, j : j + 1, ln] = got_ref[7 * i + j, l : l + 1, :]
        for k in range(5):
            vec_ref[k : k + 1, ln] = got_ref[49 + k, l : l + 1, :]
        for f in range(4):
            at = D * f + LANES * l
            gbexp_ref[at : at + LANES] = got_ref[54 + f, l, :]


def input_grad_kernel(g_ref, top_ref, bot_ref, left_ref, right_ref, cot_ref, dwk_ref, out_ref, gp):
    height, width = g_ref.shape[0], g_ref.shape[1]
    gp[HALO : HALO + height, HALO : HALO + width, :] = g_ref[...]
    gp[0:HALO, HALO : HALO + width, :] = top_ref[...]
    gp[HALO + height :, HALO : HALO + width, :] = bot_ref[...]
    gp[:, 0:HALO, :] = left_ref[...]
    gp[:, HALO + width : 2 * HALO + width, :] = right_ref[...]
    for l in range(BLOCKS):
        ln = slice(LANES * l, LANES * (l + 1))
        acc = cot_ref[:, :, ln].astype(F32)
        for j in range(7):
            s = gp[:, 6 - j : 6 - j + width, ln]
            for i in range(7):
                acc = acc + dwk_ref[i, j : j + 1, ln] * s[6 - i : 6 - i + height]
        out_ref[:, :, ln] = acc.astype(BF16)


def shifted(cells, axis, dim):
    count = lax.axis_size(axis)
    size = cells.shape[dim]
    head = lax.slice_in_dim(cells, 0, HALO, axis=dim)
    tail = lax.slice_in_dim(cells, size - HALO, size, axis=dim)
    before = lax.ppermute(tail, axis, [(i, i + 1) for i in range(count - 1)])
    after = lax.ppermute(head, axis, [(i + 1, i) for i in range(count - 1)])
    return before, after


def column_halo(cells, top, bot):
    width = cells.shape[1]
    head = jnp.concatenate([a[:, 0:HALO] for a in (top, cells, bot)], axis=0)
    tail = jnp.concatenate([a[:, width - HALO :] for a in (top, cells, bot)], axis=0)
    count = lax.axis_size("cols")
    left = lax.ppermute(tail, "cols", [(i, i + 1) for i in range(count - 1)])
    right = lax.ppermute(head, "cols", [(i + 1, i) for i in range(count - 1)])
    return left, right


def per_device(
    scale,
    feature_map,
    dw_kernel,
    dw_bias,
    layer_norm_gain,
    layer_norm_bias,
    w_expand,
    b_expand,
    w_reduce,
    b_reduce,
    layer_scale,
    cotangent,
):
    x, cot = feature_map[0], cotangent[0]
    height, width = x.shape[0], x.shape[1]
    regions = lax.axis_size("y")
    core = lax.axis_index("core").astype(jnp.int32)
    top, bot = shifted(x, "rows", 0)
    left, right = column_halo(x, top, bot)

    whole = lambda n: [pl.BlockSpec(memory_space=pltpu.VMEM)] * n
    away = lambda v: pltpu.with_memory_space_constraint(v, pltpu.HBM)
    hbm = lambda n: [pl.BlockSpec(memory_space=pltpu.HBM)] * n
    block_out, gconv, mine, send = pl.pallas_call(
        front_kernel,
        out_shape=(
            jax.ShapeDtypeStruct((height, width, D), BF16),
            jax.ShapeDtypeStruct((height, width, D), F32),
            jax.ShapeDtypeStruct((PIECES, ROWS, LANES), BF16),
            jax.ShapeDtypeStruct((PIECES, ROWS, LANES), BF16),
        ),
        in_specs=[pl.BlockSpec(memory_space=pltpu.SMEM)] + hbm(1) + whole(4) + hbm(10),
        out_specs=tuple(whole(2) + hbm(2)),
        scratch_shapes=[
            pltpu.VMEM((height, width, D), BF16),
            pltpu.VMEM((height, width, D), BF16),
            pltpu.VMEM((7, 7, D), F32),
            pltpu.VMEM((D,), F32),
            pltpu.VMEM((D,), F32),
            pltpu.VMEM((D,), F32),
            pltpu.VMEM((D, FF), BF16),
            pltpu.VMEM((FF,), F32),
            pltpu.VMEM((FF, D), BF16),
            pltpu.VMEM((D,), F32),
            pltpu.VMEM((D,), F32),
            pltpu.VMEM((height + 2 * HALO, width + 8, D), F32),
            pltpu.VMEM((height * width, D), F32),
            pltpu.VMEM((2 * height * width, FF), BF16),
            pltpu.VMEM((PIECES, 8, LANES), F32),
            pltpu.VMEM((PIECES, ROWS, LANES), BF16),
            pltpu.VMEM((PIECES, ROWS, LANES), BF16),
            pltpu.SemaphoreType.DMA((19,)),
        ],
        compiler_params=LIMIT,
        name="front",
    )(
        core.reshape(1),
        away(x),
        top,
        bot,
        left,
        right,
        away(cot),
        away(dw_kernel),
        away(dw_bias),
        away(layer_norm_gain),
        away(layer_norm_bias),
        away(w_expand),
        away(b_expand),
        away(w_reduce),
        away(b_reduce),
        away(layer_scale),
    )

    got = lax.ppermute(send, "core", [(0, 1), (1, 0)])
    gtop, gbot = shifted(gconv, "rows", 0)
    gleft, gright = column_halo(gconv, gtop, gbot)

    step = 16
    spec = pl.BlockSpec((step, ROWS, LANES), lambda i: (i, 0, 0))
    joined = pl.pallas_call(
        join_kernel,
        out_shape=jax.ShapeDtypeStruct((PIECES, ROWS, LANES), BF16),
        grid=(PIECES // step,),
        in_specs=[spec, spec],
        out_specs=spec,
        compiler_params=LIMIT,
        name="join",
    )(mine, got)
    tiles = lax.all_to_all(joined, ("rows", "cols"), 0, 0, tiled=True)
    grad_in = pl.pallas_call(
        input_grad_kernel,
        out_shape=jax.ShapeDtypeStruct((height, width, D), BF16),
        in_specs=whole(7),
        out_specs=whole(1)[0],
        scratch_shapes=[pltpu.VMEM((height + 2 * HALO, width + 8, D), F32)],
        compiler_params=LIMIT,
        name="input_grad",
    )(gconv, gtop, gbot, gleft, gright, cot, dw_kernel)
    by_region = pl.pallas_call(
        tile_sum_kernel,
        out_shape=jax.ShapeDtypeStruct((regions, FROWS + 8, LANES), F32),
        in_specs=whole(1) + hbm(1),
        out_specs=whole(1)[0],
        compiler_params=LIMIT,
        name="tile_sum",
    )(tiles, away(grad_in))
    by_region = lax.all_to_all(by_region, "y", 0, 0, tiled=True)
    grad_expand, grad_reduce_t, small = pl.pallas_call(
        functools.partial(region_sum_kernel, scale),
        out_shape=(
            jax.ShapeDtypeStruct((DROWS, FROWS), F32),
            jax.ShapeDtypeStruct((DROWS, FROWS), F32),
            jax.ShapeDtypeStruct((PIECES, BLOCKS, LANES), F32),
        ),
        in_specs=whole(1),
        out_specs=tuple(whole(3)),
        compiler_params=LIMIT,
        name="region_sum",
    )(by_region)
    small = lax.all_to_all(small, ("rows", "cols"), 0, 0, tiled=True)
    gker, vectors, gbexp = pl.pallas_call(
        spread_kernel,
        out_shape=(
            jax.ShapeDtypeStruct((7, 7, D), F32),
            jax.ShapeDtypeStruct((5, D), F32),
            jax.ShapeDtypeStruct((FF,), F32),
        ),
        in_specs=whole(1),
        out_specs=tuple(whole(3)),
        compiler_params=LIMIT,
        name="spread",
    )(small)
    return (
        block_out[None],
        grad_in[None],
        grad_expand,
        grad_reduce_t,
        gker,
        vectors,
        gbexp,
    )


def solution(mesh):
    shape = dict(mesh.shape)
    fine = Mesh(
        mesh.devices.reshape(shape["rows"], shape["cols"], shape["rep"] // 2, 2),
        ("rows", "cols", "y", "core"),
    )
    tile = P(("y", "core"), "rows", "cols", None)
    grad = P(("y", "core"), ("rows", "cols"))
    pixels = 16 * 64 * 128
    scale = float(pixels) ** -0.5
    return jax.shard_map(
        functools.partial(per_device, scale),
        mesh=fine,
        in_specs=(tile,) + (P(),) * 9 + (tile,),
        out_specs=(tile, tile, grad, grad, P(), P(), P()),
        check_vma=False,
    )
```

```python
import functools

import jax
import jax.numpy as jnp
from jax import lax
from jax.experimental import pallas as pl
from jax.experimental.pallas import tpu as pltpu
from jax.sharding import Mesh
from jax.sharding import PartitionSpec as P

EPS = 1e-06
INV_ROOT_TWO = 0.7071067811865476
INV_ROOT_TWO_PI = 0.3989422804014327
F32 = jnp.float32
BF16 = jnp.bfloat16
D = 384
FF = 1536
LANES = 128
BLOCKS = D // LANES
HALO = 3
FROWS = 24
DROWS = 24
PIECES = 8
FAR = 64
BIG = BLOCKS * 8 * FROWS
SHARE = 12
ROWS = BIG + 2 * SHARE
TALL = ("zh", "zl")
WIDE = ("xh", "xl")
LIMIT = pltpu.CompilerParams(vmem_limit_bytes=50 * 1024 * 1024)


def matmul(a, b, ca, cb):
    return lax.dot_general(a, b, (((ca,), (cb,)), ((), ())), preferred_element_type=F32)


def front_kernel(
    core_ref,
    x_hbm,
    top_ref,
    bot_ref,
    left_ref,
    right_ref,
    cot_hbm,
    dwk_hbm,
    dwb_hbm,
    gain_hbm,
    lnb_hbm,
    wexp_hbm,
    bexp_hbm,
    wred_hbm,
    bred_hbm,
    ls_hbm,
    block_ref,
    gconv_ref,
    mine_hbm,
    send_hbm,
    x_ref,
    cot_ref,
    dwk_ref,
    dwb_ref,
    gain_ref,
    lnb_ref,
    wexp_ref,
    bexp_ref,
    wred_ref,
    bred_ref,
    ls_ref,
    xp,
    conv,
    both,
    small,
    mine_ref,
    send_ref,
    sems,
):
    pairs = (
        (x_hbm, x_ref),
        (dwk_hbm, dwk_ref),
        (dwb_hbm, dwb_ref),
        (gain_hbm, gain_ref),
        (lnb_hbm, lnb_ref),
        (cot_hbm, cot_ref),
        (ls_hbm, ls_ref),
        (bexp_hbm, bexp_ref),
        (bred_hbm, bred_ref),
        (wexp_hbm, wexp_ref),
        (wred_hbm, wred_ref),
    )
    copies = [pltpu.make_async_copy(a, b, sems.at[k]) for k, (a, b) in enumerate(pairs)]
    for c in copies:
        c.start()
    height, width = x_ref.shape[0], x_ref.shape[1]
    pixels = height * width
    row = lambda ref: ref[...].reshape(1, -1)
    xp[0:HALO, HALO : HALO + width, :] = top_ref[...].astype(F32)
    xp[HALO + height :, HALO : HALO + width, :] = bot_ref[...].astype(F32)
    xp[:, 0:HALO, :] = left_ref[...].astype(F32)
    xp[:, HALO + width : 2 * HALO + width, :] = right_ref[...].astype(F32)
    small[...] = jnp.zeros_like(small)

    def put(p, l, value):
        at = BLOCKS * (p % 4) + l
        small[p // 4, at : at + 1, :] = value

    for c in copies[0:2]:
        c.wait()
    xp[HALO : HALO + height, HALO : HALO + width, :] = x_ref[...].astype(F32)
    for l in range(BLOCKS):
        ln = slice(LANES * l, LANES * (l + 1))
        acc = jnp.zeros((height, width, LANES), F32)
        for j in range(7):
            s = xp[:, j : j + width, ln]
            for i in range(7):
                acc = acc + dwk_ref[i, j : j + 1, ln] * s[i : i + height]
        conv[:, ln] = acc.reshape(pixels, LANES)
    for c in copies[2:]:
        c.wait()
    flat = conv[...] + row(dwb_ref)
    centered = flat - jnp.mean(flat, axis=-1, keepdims=True)
    inv = lax.rsqrt(jnp.mean(centered * centered, axis=-1, keepdims=True) + EPS)
    xhat = centered * inv
    gain = row(gain_ref)
    normed = (xhat * gain + row(lnb_ref)).astype(BF16)
    grad = cot_ref[...].astype(F32).reshape(pixels, D)
    scaled = grad * row(ls_ref)
    g_branch = scaled.astype(BF16)
    for f in range(4):
        sl = slice(D * f, D * (f + 1))
        pre = matmul(normed, wexp_ref[:, sl], 1, 0) + bexp_ref[sl].reshape(1, D)
        cdf = 0.5 * (1.0 + lax.erf(pre * INV_ROOT_TWO))
        pdf = jnp.exp(-0.5 * pre * pre) * INV_ROOT_TWO_PI
        g_act = matmul(g_branch, wred_ref[sl, :], 1, 1)
        g_pre = g_act * (cdf + pre * pdf)
        both[0:pixels, sl] = g_pre.astype(BF16)
        both[pixels : 2 * pixels, sl] = (pre * cdf).astype(BF16)
        total = jnp.sum(g_pre, axis=0, keepdims=True)
        for l in range(BLOCKS):
            put(54 + f, l, total[:, LANES * l : LANES * (l + 1)])
    branch = matmul(both[pixels : 2 * pixels, :], wred_ref[...], 1, 0) + row(bred_ref)
    block = x_ref[...].astype(F32).reshape(pixels, D) + row(ls_ref) * branch
    block_ref[...] = block.astype(BF16).reshape(height, width, D)
    g_norm = matmul(both[0:pixels, :], wexp_ref[...], 1, 1)
    gx = g_norm * gain
    gconv = inv * (
        gx
        - jnp.mean(gx, axis=-1, keepdims=True)
        - xhat * jnp.mean(gx * xhat, axis=-1, keepdims=True)
    )
    gconv_ref[...] = gconv.reshape(height, width, D)
    sums = (gconv, g_norm * xhat, g_norm, scaled, grad * branch)
    for k, value in enumerate(sums):
        total = jnp.sum(value, axis=0, keepdims=True)
        for l in range(BLOCKS):
            put(49 + k, l, total[:, LANES * l : LANES * (l + 1)])
    for l in range(BLOCKS):
        ln = slice(LANES * l, LANES * (l + 1))
        g3 = gconv_ref[:, :, ln]
        for j in range(7):
            s = xp[:, j : j + width, ln]
            for i in range(7):
                part = jnp.sum(g3 * s[i : i + height], axis=0)
                put(7 * i + j, l, jnp.sum(part, axis=0, keepdims=True))
    value = small[:, 0:SHARE, :]
    small[:, SHARE : 2 * SHARE, :] = value - value.astype(BF16).astype(F32)
    chan = lax.broadcasted_iota(jnp.int32, (D, D), 0)
    column = lax.broadcasted_iota(jnp.int32, (1, D), 1)
    half = (column >= D // 2).astype(jnp.int32)
    rest = column - (D // 2) * half
    block = (rest * 1366) >> 16
    inside = rest - 2 * DROWS * block
    of_e = inside < DROWS
    base = 4 * DROWS * block + jnp.where(of_e, inside, inside - DROWS)
    pixel = lax.broadcasted_iota(jnp.int32, (2 * pixels, 1), 0)
    keep = jnp.where(pixel < pixels, 1, 0) == jnp.where(of_e, 1, 0)
    stack = jnp.concatenate([normed, g_branch], axis=0)
    lane = lax.broadcasted_iota(jnp.int32, (1, 1, LANES), 2)
    outputs = []

    def flush(out, hbm, rows):
        c = pltpu.make_async_copy(out.at[:, rows], hbm.at[:, rows], sems.at[11 + len(outputs)])
        c.start()
        outputs.append(c)

    for which, (out, hbm) in enumerate(((send_ref, send_hbm), (mine_ref, mine_hbm))):
        core = core_ref[0] if which == 1 else 1 - core_ref[0]
        out[:, BIG:ROWS, :] = small[pl.ds(PIECES * core, PIECES)].astype(BF16)
        flush(out, hbm, slice(BIG, ROWS))
        right = []
        for order in range(2):
            turn = half if order == 0 else 1 - half
            pick = (chan == base + 2 * DROWS * turn + DROWS * core).astype(F32).astype(BF16)
            right.append(jnp.where(keep, matmul(stack, pick, 1, 0), 0.0).astype(BF16))
        for low in range(2):
            g = []
            for order in range(2):
                f = low + 2 * order
                part = matmul(both[:, D * f : D * (f + 1)], right[order], 0, 0)
                g.append(part.reshape(2, 4, 2, FROWS, D))
            for zl in range(2):
                for xl in range(2):
                    for yl in range(2):
                        one, two = g[yl][zl, :, xl], g[1 - yl][zl, :, xl]
                        pieces = (
                            one[:, :, 0:LANES],
                            jnp.where(
                                lane < LANES // 2,
                                one[:, :, LANES : 2 * LANES],
                                two[:, :, LANES : 2 * LANES],
                            ),
                            two[:, :, 2 * LANES : D],
                        )
                        for l, piece in enumerate(pieces):
                            at = 8 * FROWS * l + 4 * FROWS * low
                            out[4 * zl + 2 * xl + yl, at : at + 4 * FROWS, :] = piece.reshape(
                                4 * FROWS, LANES
                            ).astype(BF16)
            for l in range(BLOCKS):
                at = 8 * FROWS * l + 4 * FROWS * low
                flush(out, hbm, slice(at, at + 4 * FROWS))
    for c in outputs:
        c.wait()


def join_kernel(mine_ref, got_ref, top_hbm, bot_hbm, out_ref):
    big = mine_ref[:, 0:BIG, :].astype(F32) + got_ref[:, 0:BIG, :].astype(F32)
    out_ref[:, 0:BIG, :] = big.astype(BF16)
    both = mine_ref[:, BIG:ROWS, :].astype(F32) + got_ref[:, BIG:ROWS, :].astype(F32)
    value = both[:, 0:SHARE] + both[:, SHARE : 2 * SHARE]
    low = value - value.astype(BF16).astype(F32)
    out_ref[:, BIG:ROWS, :] = jnp.concatenate([value, low], axis=1).astype(BF16)


def block_sum_kernel(yl_ref, got_ref, left_hbm, right_hbm, out_ref, total):
    total[...] = jnp.sum(got_ref[...].astype(F32), axis=0)
    small = total[BIG : BIG + SHARE, :] + total[BIG + SHARE : ROWS, :]
    side = LANES // 2
    folded = jnp.concatenate([small[:, 0:side], small[:, side:]], axis=0)
    gap = jnp.zeros((FROWS, side - 2 * DROWS), F32)
    tail = jnp.concatenate([gap, folded], axis=1)
    for low in range(2):
        for xh in range(4):
            at = 4 * FROWS * low + FROWS * xh
            wide = jnp.concatenate(
                [
                    total[8 * FROWS * l + at : 8 * FROWS * l + at + FROWS, :]
                    for l in range(BLOCKS)
                ],
                axis=1,
            )
            for half in range(2):
                turn = yl_ref[0] if half == 0 else 1 - yl_ref[0]
                zh = low + 2 * turn
                for yh in range(4):
                    start = D // 2 * half + 2 * DROWS * yh
                    piece = jnp.concatenate([wide[:, start : start + 2 * DROWS], tail], axis=1)
                    out_ref[16 * zh + 4 * xh + yh] = piece.astype(BF16)


def far_sum_kernel(scale, got_ref, ge_ref, gr_ref, small_ref):
    total = jnp.sum(got_ref[...].astype(F32), axis=0) * scale
    turned = jnp.transpose(total, (1, 0))
    ge_ref[...] = turned[0:DROWS, 0:FROWS]
    gr_ref[...] = turned[DROWS : 2 * DROWS, 0:FROWS]
    side = LANES // 2
    small = jnp.concatenate([total[0:SHARE, side:], total[SHARE:FROWS, side:]], axis=1)
    small_ref[...] = jnp.broadcast_to(small, small_ref.shape)


def spread_kernel(got_ref, gker_ref, vec_ref, gbexp_ref):
    def take(p, l):
        share, at = p // 4, BLOCKS * (p % 4) + l
        return got_ref[2 * (share % PIECES) + share // PIECES, at : at + 1, :]

    for l in range(BLOCKS):
        ln = slice(LANES * l, LANES * (l + 1))
        for i in range(7):
            for j in range(7):
                gker_ref[i, j : j + 1, ln] = take(7 * i + j, l)
        for k in range(5):
            vec_ref[k : k + 1, ln] = take(49 + k, l)
        for f in range(4):
            at = D * f + LANES * l
            gbexp_ref[at : at + LANES] = take(54 + f, l).reshape(LANES)


def input_grad_kernel(g_ref, top_ref, bot_ref, left_ref, right_ref, cot_ref, dwk_ref, out_ref, gp):
    height, width = g_ref.shape[0], g_ref.shape[1]
    gp[HALO : HALO + height, HALO : HALO + width, :] = g_ref[...]
    gp[0:HALO, HALO : HALO + width, :] = top_ref[...]
    gp[HALO + height :, HALO : HALO + width, :] = bot_ref[...]
    gp[:, 0:HALO, :] = left_ref[...]
    gp[:, HALO + width : 2 * HALO + width, :] = right_ref[...]
    for l in range(BLOCKS):
        ln = slice(LANES * l, LANES * (l + 1))
        acc = cot_ref[:, :, ln].astype(F32)
        for j in range(7):
            s = gp[:, 6 - j : 6 - j + width, ln]
            for i in range(7):
                acc = acc + dwk_ref[i, j : j + 1, ln] * s[6 - i : 6 - i + height]
        out_ref[:, :, ln] = acc.astype(BF16)


def shifted(cells, axis, dim):
    count = lax.axis_size(axis)
    size = cells.shape[dim]
    head = lax.slice_in_dim(cells, 0, HALO, axis=dim)
    tail = lax.slice_in_dim(cells, size - HALO, size, axis=dim)
    before = lax.ppermute(tail, axis, [(i, i + 1) for i in range(count - 1)])
    after = lax.ppermute(head, axis, [(i + 1, i) for i in range(count - 1)])
    return before, after


def column_halo(cells, top, bot):
    width = cells.shape[1]
    head = jnp.concatenate([a[:, 0:HALO] for a in (top, cells, bot)], axis=0)
    tail = jnp.concatenate([a[:, width - HALO :] for a in (top, cells, bot)], axis=0)
    count = lax.axis_size(WIDE)
    left = lax.ppermute(tail, WIDE, [(i, i + 1) for i in range(count - 1)])
    right = lax.ppermute(head, WIDE, [(i + 1, i) for i in range(count - 1)])
    return left, right


def per_device(
    scale,
    feature_map,
    dw_kernel,
    dw_bias,
    layer_norm_gain,
    layer_norm_bias,
    w_expand,
    b_expand,
    w_reduce,
    b_reduce,
    layer_scale,
    cotangent,
):
    x, cot = feature_map[0], cotangent[0]
    height, width = x.shape[0], x.shape[1]
    core = lax.axis_index("core").astype(jnp.int32)
    yl = lax.axis_index("yl").astype(jnp.int32)
    top, bot = shifted(x, TALL, 0)
    left, right = column_halo(x, top, bot)

    whole = lambda n: [pl.BlockSpec(memory_space=pltpu.VMEM)] * n
    away = lambda v: pltpu.with_memory_space_constraint(v, pltpu.HBM)
    hbm = lambda n: [pl.BlockSpec(memory_space=pltpu.HBM)] * n
    block_out, gconv, mine, send = pl.pallas_call(
        front_kernel,
        out_shape=(
            jax.ShapeDtypeStruct((height, width, D), BF16),
            jax.ShapeDtypeStruct((height, width, D), F32),
            jax.ShapeDtypeStruct((PIECES, ROWS, LANES), BF16),
            jax.ShapeDtypeStruct((PIECES, ROWS, LANES), BF16),
        ),
        in_specs=[pl.BlockSpec(memory_space=pltpu.SMEM)] + hbm(1) + whole(4) + hbm(10),
        out_specs=tuple(whole(2) + hbm(2)),
        scratch_shapes=[
            pltpu.VMEM((height, width, D), BF16),
            pltpu.VMEM((height, width, D), BF16),
            pltpu.VMEM((7, 7, D), F32),
            pltpu.VMEM((D,), F32),
            pltpu.VMEM((D,), F32),
            pltpu.VMEM((D,), F32),
            pltpu.VMEM((D, FF), BF16),
            pltpu.VMEM((FF,), F32),
            pltpu.VMEM((FF, D), BF16),
            pltpu.VMEM((D,), F32),
            pltpu.VMEM((D,), F32),
            pltpu.VMEM((height + 2 * HALO, width + 8, D), F32),
            pltpu.VMEM((height * width, D), F32),
            pltpu.VMEM((2 * height * width, FF), BF16),
            pltpu.VMEM((2 * PIECES, 2 * SHARE, LANES), F32),
            pltpu.VMEM((PIECES, ROWS, LANES), BF16),
            pltpu.VMEM((PIECES, ROWS, LANES), BF16),
            pltpu.SemaphoreType.DMA((25,)),
        ],
        compiler_params=LIMIT,
        name="front",
    )(
        core.reshape(1),
        away(x),
        top,
        bot,
        left,
        right,
        away(cot),
        away(dw_kernel),
        away(dw_bias),
        away(layer_norm_gain),
        away(layer_norm_bias),
        away(w_expand),
        away(b_expand),
        away(w_reduce),
        away(b_reduce),
        away(layer_scale),
    )

    got = lax.ppermute(send, "core", [(0, 1), (1, 0)])
    gtop, gbot = shifted(gconv, TALL, 0)
    gleft, gright = column_halo(gconv, gtop, gbot)

    step = 2
    spec = pl.BlockSpec((step, ROWS, LANES), lambda i: (i, 0, 0))
    free = lambda n: [pl.BlockSpec(memory_space=pl.ANY)] * n
    smem = [pl.BlockSpec(memory_space=pltpu.SMEM)]
    joined = pl.pallas_call(
        join_kernel,
        out_shape=jax.ShapeDtypeStruct((PIECES, ROWS, LANES), BF16),
        grid=(PIECES // step,),
        in_specs=[spec, spec] + free(2),
        out_specs=spec,
        compiler_params=LIMIT,
        name="join",
    )(mine, got, gtop, gbot)
    near = lax.all_to_all(joined, ("zl", "xl", "yl"), 0, 0, tiled=True)
    by_block = pl.pallas_call(
        block_sum_kernel,
        out_shape=jax.ShapeDtypeStruct((FAR, FROWS, LANES), BF16),
        in_specs=smem + whole(1) + free(2),
        out_specs=whole(1)[0],
        scratch_shapes=[pltpu.VMEM((ROWS, LANES), F32)],
        compiler_params=LIMIT,
        name="block_sum",
    )(yl.reshape(1), near, gleft, gright)
    grad_in = pl.pallas_call(
        input_grad_kernel,
        out_shape=jax.ShapeDtypeStruct((height, width, D), BF16),
        in_specs=whole(7),
        out_specs=whole(1)[0],
        scratch_shapes=[pltpu.VMEM((height + 2 * HALO, width + 8, D), F32)],
        compiler_params=LIMIT,
        name="input_grad",
    )(gconv, gtop, gbot, gleft, gright, cot, dw_kernel)
    by_block = lax.all_to_all(by_block, ("zh", "xh", "yh"), 0, 0, tiled=True)
    grad_expand, grad_reduce_t, small = pl.pallas_call(
        functools.partial(far_sum_kernel, scale),
        out_shape=(
            jax.ShapeDtypeStruct((DROWS, FROWS), F32),
            jax.ShapeDtypeStruct((DROWS, FROWS), F32),
            jax.ShapeDtypeStruct((2 * PIECES, SHARE, LANES), F32),
        ),
        in_specs=whole(1),
        out_specs=tuple(whole(3)),
        compiler_params=LIMIT,
        name="far_sum",
    )(by_block)
    small = lax.all_to_all(small, ("zl", "xl", "yl", "core"), 0, 0, tiled=True)
    gker, vectors, gbexp = pl.pallas_call(
        spread_kernel,
        out_shape=(
            jax.ShapeDtypeStruct((7, 7, D), F32),
            jax.ShapeDtypeStruct((5, D), F32),
            jax.ShapeDtypeStruct((FF,), F32),
        ),
        in_specs=whole(1),
        out_specs=tuple(whole(3)),
        compiler_params=LIMIT,
        name="spread",
    )(small)
    return (
        block_out[None],
        grad_in[None],
        grad_expand,
        grad_reduce_t,
        gker,
        vectors,
        gbexp,
    )


def solution(mesh):
    shape = dict(mesh.shape)
    sizes = (shape["rows"] // 2, 2, shape["cols"] // 2, 2, shape["rep"] // 4, 2, 2)
    fine = Mesh(mesh.devices.reshape(sizes), TALL + WIDE + ("yh", "yl", "core"))
    tile = P(("yh", "yl", "core"), TALL, WIDE, None)
    grad = P(("yh", "yl", "core"), TALL + WIDE)
    pixels = 16 * 64 * 128
    scale = float(pixels) ** -0.5
    return jax.shard_map(
        functools.partial(per_device, scale),
        mesh=fine,
        in_specs=(tile,) + (P(),) * 9 + (tile,),
        out_specs=(tile, tile, grad, grad, P(), P(), P()),
        check_vma=False,
    )
```

```python
import functools

import jax
import jax.numpy as jnp
from jax import lax
from jax.experimental import pallas as pl
from jax.experimental.pallas import tpu as pltpu
from jax.sharding import Mesh
from jax.sharding import PartitionSpec as P

EPS = 1e-06
INV_ROOT_TWO = 0.7071067811865476
INV_ROOT_TWO_PI = 0.3989422804014327
F32 = jnp.float32
BF16 = jnp.bfloat16
D = 384
FF = 1536
LANES = 128
BLOCKS = D // LANES
HALO = 3
FROWS = 24
DROWS = 24
PIECES = 8
BIG = BLOCKS * 8 * FROWS
SHARE = 12
ROWS = BIG + 2 * SHARE
TALL = ("zh", "zm", "zl")
WIDE = ("xh", "xm", "xl")
DEEP = ("yh", "ym", "yl", "core")
LIMIT = pltpu.CompilerParams(vmem_limit_bytes=50 * 1024 * 1024)


def matmul(a, b, ca, cb):
    return lax.dot_general(a, b, (((ca,), (cb,)), ((), ())), preferred_element_type=F32)


def front_kernel(
    core_ref,
    x_hbm,
    top_ref,
    bot_ref,
    left_ref,
    right_ref,
    cot_hbm,
    dwk_hbm,
    dwb_hbm,
    gain_hbm,
    lnb_hbm,
    wexp_hbm,
    bexp_hbm,
    wred_hbm,
    bred_hbm,
    ls_hbm,
    block_ref,
    gconv_ref,
    mine_hbm,
    send_hbm,
    x_ref,
    cot_ref,
    dwk_ref,
    dwb_ref,
    gain_ref,
    lnb_ref,
    wexp_ref,
    bexp_ref,
    wred_ref,
    bred_ref,
    ls_ref,
    xp,
    conv,
    both,
    small,
    mine_ref,
    send_ref,
    sems,
):
    pairs = (
        (x_hbm, x_ref),
        (dwk_hbm, dwk_ref),
        (dwb_hbm, dwb_ref),
        (gain_hbm, gain_ref),
        (lnb_hbm, lnb_ref),
        (cot_hbm, cot_ref),
        (ls_hbm, ls_ref),
        (bexp_hbm, bexp_ref),
        (bred_hbm, bred_ref),
        (wexp_hbm, wexp_ref),
        (wred_hbm, wred_ref),
    )
    copies = [pltpu.make_async_copy(a, b, sems.at[k]) for k, (a, b) in enumerate(pairs)]
    for c in copies:
        c.start()
    height, width = x_ref.shape[0], x_ref.shape[1]
    pixels = height * width
    row = lambda ref: ref[...].reshape(1, -1)
    xp[0:HALO, HALO : HALO + width, :] = top_ref[...].astype(F32)
    xp[HALO + height :, HALO : HALO + width, :] = bot_ref[...].astype(F32)
    xp[:, 0:HALO, :] = left_ref[...].astype(F32)
    xp[:, HALO + width : 2 * HALO + width, :] = right_ref[...].astype(F32)
    small[...] = jnp.zeros_like(small)

    def put(p, l, value):
        at = BLOCKS * (p % 4) + l
        small[p // 4, at : at + 1, :] = value

    for c in copies[0:2]:
        c.wait()
    xp[HALO : HALO + height, HALO : HALO + width, :] = x_ref[...].astype(F32)
    for l in range(BLOCKS):
        ln = slice(LANES * l, LANES * (l + 1))
        acc = jnp.zeros((height, width, LANES), F32)
        for j in range(7):
            s = xp[:, j : j + width, ln]
            for i in range(7):
                acc = acc + dwk_ref[i, j : j + 1, ln] * s[i : i + height]
        conv[:, ln] = acc.reshape(pixels, LANES)
    for c in copies[2:]:
        c.wait()
    flat = conv[...] + row(dwb_ref)
    centered = flat - jnp.mean(flat, axis=-1, keepdims=True)
    inv = lax.rsqrt(jnp.mean(centered * centered, axis=-1, keepdims=True) + EPS)
    xhat = centered * inv
    gain = row(gain_ref)
    normed = (xhat * gain + row(lnb_ref)).astype(BF16)
    grad = cot_ref[...].astype(F32).reshape(pixels, D)
    scaled = grad * row(ls_ref)
    g_branch = scaled.astype(BF16)
    for f in range(4):
        sl = slice(D * f, D * (f + 1))
        pre = matmul(normed, wexp_ref[:, sl], 1, 0) + bexp_ref[sl].reshape(1, D)
        cdf = 0.5 * (1.0 + lax.erf(pre * INV_ROOT_TWO))
        pdf = jnp.exp(-0.5 * pre * pre) * INV_ROOT_TWO_PI
        g_act = matmul(g_branch, wred_ref[sl, :], 1, 1)
        g_pre = g_act * (cdf + pre * pdf)
        both[0:pixels, sl] = g_pre.astype(BF16)
        both[pixels : 2 * pixels, sl] = (pre * cdf).astype(BF16)
        total = jnp.sum(g_pre, axis=0, keepdims=True)
        for l in range(BLOCKS):
            put(54 + f, l, total[:, LANES * l : LANES * (l + 1)])
    branch = matmul(both[pixels : 2 * pixels, :], wred_ref[...], 1, 0) + row(bred_ref)
    block = x_ref[...].astype(F32).reshape(pixels, D) + row(ls_ref) * branch
    block_ref[...] = block.astype(BF16).reshape(height, width, D)
    g_norm = matmul(both[0:pixels, :], wexp_ref[...], 1, 1)
    gx = g_norm * gain
    gconv = inv * (
        gx
        - jnp.mean(gx, axis=-1, keepdims=True)
        - xhat * jnp.mean(gx * xhat, axis=-1, keepdims=True)
    )
    gconv_ref[...] = gconv.reshape(height, width, D)
    sums = (gconv, g_norm * xhat, g_norm, scaled, grad * branch)
    for k, value in enumerate(sums):
        total = jnp.sum(value, axis=0, keepdims=True)
        for l in range(BLOCKS):
            put(49 + k, l, total[:, LANES * l : LANES * (l + 1)])
    for l in range(BLOCKS):
        ln = slice(LANES * l, LANES * (l + 1))
        g3 = gconv_ref[:, :, ln]
        for j in range(7):
            s = xp[:, j : j + width, ln]
            for i in range(7):
                part = jnp.sum(g3 * s[i : i + height], axis=0)
                put(7 * i + j, l, jnp.sum(part, axis=0, keepdims=True))
    value = small[:, 0:SHARE, :]
    small[:, SHARE : 2 * SHARE, :] = value - value.astype(BF16).astype(F32)
    chan = lax.broadcasted_iota(jnp.int32, (D, D), 0)
    column = lax.broadcasted_iota(jnp.int32, (1, D), 1)
    half = (column >= D // 2).astype(jnp.int32)
    rest = column - (D // 2) * half
    block = (rest * 1366) >> 16
    inside = rest - 2 * DROWS * block
    of_e = inside < DROWS
    base = 4 * DROWS * block + jnp.where(of_e, inside, inside - DROWS)
    pixel = lax.broadcasted_iota(jnp.int32, (2 * pixels, 1), 0)
    keep = jnp.where(pixel < pixels, 1, 0) == jnp.where(of_e, 1, 0)
    stack = jnp.concatenate([normed, g_branch], axis=0)
    lane = lax.broadcasted_iota(jnp.int32, (1, 1, LANES), 2)
    outputs = []

    def flush(out, hbm, rows):
        c = pltpu.make_async_copy(out.at[:, rows], hbm.at[:, rows], sems.at[11 + len(outputs)])
        c.start()
        outputs.append(c)

    for which, (out, hbm) in enumerate(((send_ref, send_hbm), (mine_ref, mine_hbm))):
        core = core_ref[0] if which == 1 else 1 - core_ref[0]
        out[:, BIG:ROWS, :] = small[pl.ds(PIECES * core, PIECES)].astype(BF16)
        flush(out, hbm, slice(BIG, ROWS))
        right = []
        for order in range(2):
            turn = half if order == 0 else 1 - half
            pick = (chan == base + 2 * DROWS * turn + DROWS * core).astype(F32).astype(BF16)
            right.append(jnp.where(keep, matmul(stack, pick, 1, 0), 0.0).astype(BF16))
        for low in range(2):
            g = []
            for order in range(2):
                f = low + 2 * order
                part = matmul(both[:, D * f : D * (f + 1)], right[order], 0, 0)
                g.append(part.reshape(2, 4, 2, FROWS, D))
            for zl in range(2):
                for xl in range(2):
                    for yl in range(2):
                        one, two = g[yl][zl, :, xl], g[1 - yl][zl, :, xl]
                        pieces = (
                            one[:, :, 0:LANES],
                            jnp.where(
                                lane < LANES // 2,
                                one[:, :, LANES : 2 * LANES],
                                two[:, :, LANES : 2 * LANES],
                            ),
                            two[:, :, 2 * LANES : D],
                        )
                        for l, piece in enumerate(pieces):
                            at = 8 * FROWS * l + 4 * FROWS * low
                            out[4 * zl + 2 * xl + yl, at : at + 4 * FROWS, :] = piece.reshape(
                                4 * FROWS, LANES
                            ).astype(BF16)
            for l in range(BLOCKS):
                at = 8 * FROWS * l + 4 * FROWS * low
                flush(out, hbm, slice(at, at + 4 * FROWS))
    for c in outputs:
        c.wait()


def join_kernel(mine_ref, got_ref, top_hbm, bot_hbm, out_ref):
    big = mine_ref[:, 0:BIG, :].astype(F32) + got_ref[:, 0:BIG, :].astype(F32)
    out_ref[:, 0:BIG, :] = big.astype(BF16)
    both = mine_ref[:, BIG:ROWS, :].astype(F32) + got_ref[:, BIG:ROWS, :].astype(F32)
    value = both[:, 0:SHARE] + both[:, SHARE : 2 * SHARE]
    low = value - value.astype(BF16).astype(F32)
    out_ref[:, BIG:ROWS, :] = jnp.concatenate([value, low], axis=1).astype(BF16)


def block_sum_kernel(got_ref, left_hbm, right_hbm, out_ref, total):
    total[...] = jnp.sum(got_ref[...].astype(F32), axis=0)
    small = total[BIG : BIG + SHARE, :] + total[BIG + SHARE : ROWS, :]
    high = small.astype(BF16).astype(F32)
    both = jnp.concatenate([high, small - high], axis=0)
    width = LANES - 4 * DROWS
    for zm in range(2):
        for xh in range(2):
            for xm in range(2):
                at = 4 * FROWS * zm + FROWS * (2 * xh + xm)
                wide = jnp.concatenate(
                    [
                        total[8 * FROWS * l + at : 8 * FROWS * l + at + FROWS, :]
                        for l in range(BLOCKS)
                    ],
                    axis=1,
                )
                for half in range(2):
                    group = 2 * half + xh
                    tail = both[:, width * group : width * (group + 1)]
                    for ym in range(2):
                        start = D // 2 * half + 2 * DROWS * ym
                        piece = jnp.concatenate(
                            [
                                wide[:, start : start + 2 * DROWS],
                                wide[:, start + 4 * DROWS : start + 6 * DROWS],
                                tail,
                            ],
                            axis=1,
                        )
                        rows = slice(FROWS * group, FROWS * (group + 1))
                        out_ref[4 * zm + 2 * xm + ym, rows, :] = piece.astype(BF16)


def middle_sum_kernel(yl_ref, got_ref, out_ref):
    total = jnp.sum(got_ref[...].astype(F32), axis=0)
    both = jnp.concatenate(
        [total[FROWS * k : FROWS * (k + 1), 4 * DROWS :] for k in range(4)], axis=1
    )
    small = both[0:SHARE] + both[SHARE : 2 * SHARE]
    side = LANES // 2
    folded = jnp.concatenate([small[:, 0:side], small[:, side:]], axis=0)
    gap = jnp.zeros((FROWS, side - 2 * DROWS), F32)
    for half in range(2):
        zh = yl_ref[0] if half == 0 else 1 - yl_ref[0]
        for xh in range(2):
            rows = slice(FROWS * (2 * half + xh), FROWS * (2 * half + xh + 1))
            for yh in range(2):
                own = total[rows, 2 * DROWS * yh : 2 * DROWS * (yh + 1)]
                out_ref[4 * zh + 2 * xh + yh] = jnp.concatenate([own, gap, folded], axis=1)


def far_sum_kernel(scale, got_ref, ge_ref, gr_ref, small_ref):
    total = jnp.sum(got_ref[...], axis=0) * scale
    turned = jnp.transpose(total, (1, 0))
    ge_ref[...] = turned[0:DROWS, 0:FROWS]
    gr_ref[...] = turned[DROWS : 2 * DROWS, 0:FROWS]
    side = LANES // 2
    small = jnp.concatenate([total[0:SHARE, side:], total[SHARE:FROWS, side:]], axis=1)
    small_ref[...] = jnp.broadcast_to(small, small_ref.shape)


def spread_kernel(got_ref, gker_ref, vec_ref, gbexp_ref):
    def take(p, l):
        share, at = p // 4, BLOCKS * (p % 4) + l
        return got_ref[2 * (share % PIECES) + share // PIECES, at : at + 1, :]

    for l in range(BLOCKS):
        ln = slice(LANES * l, LANES * (l + 1))
        for i in range(7):
            for j in range(7):
                gker_ref[i, j : j + 1, ln] = take(7 * i + j, l)
        for k in range(5):
            vec_ref[k : k + 1, ln] = take(49 + k, l)
        for f in range(4):
            at = D * f + LANES * l
            gbexp_ref[at : at + LANES] = take(54 + f, l).reshape(LANES)


def input_grad_kernel(g_ref, top_ref, bot_ref, left_ref, right_ref, cot_ref, dwk_ref, out_ref, gp):
    height, width = g_ref.shape[0], g_ref.shape[1]
    gp[HALO : HALO + height, HALO : HALO + width, :] = g_ref[...]
    gp[0:HALO, HALO : HALO + width, :] = top_ref[...]
    gp[HALO + height :, HALO : HALO + width, :] = bot_ref[...]
    gp[:, 0:HALO, :] = left_ref[...]
    gp[:, HALO + width : 2 * HALO + width, :] = right_ref[...]
    for l in range(BLOCKS):
        ln = slice(LANES * l, LANES * (l + 1))
        acc = cot_ref[:, :, ln].astype(F32)
        for j in range(7):
            s = gp[:, 6 - j : 6 - j + width, ln]
            for i in range(7):
                acc = acc + dwk_ref[i, j : j + 1, ln] * s[6 - i : 6 - i + height]
        out_ref[:, :, ln] = acc.astype(BF16)


def shifted(cells, axis, dim):
    count = lax.axis_size(axis)
    size = cells.shape[dim]
    head = lax.slice_in_dim(cells, 0, HALO, axis=dim)
    tail = lax.slice_in_dim(cells, size - HALO, size, axis=dim)
    before = lax.ppermute(tail, axis, [(i, i + 1) for i in range(count - 1)])
    after = lax.ppermute(head, axis, [(i + 1, i) for i in range(count - 1)])
    return before, after


def column_halo(cells, top, bot):
    width = cells.shape[1]
    head = jnp.concatenate([a[:, 0:HALO] for a in (top, cells, bot)], axis=0)
    tail = jnp.concatenate([a[:, width - HALO :] for a in (top, cells, bot)], axis=0)
    count = lax.axis_size(WIDE)
    left = lax.ppermute(tail, WIDE, [(i, i + 1) for i in range(count - 1)])
    right = lax.ppermute(head, WIDE, [(i + 1, i) for i in range(count - 1)])
    return left, right


def per_device(
    scale,
    feature_map,
    dw_kernel,
    dw_bias,
    layer_norm_gain,
    layer_norm_bias,
    w_expand,
    b_expand,
    w_reduce,
    b_reduce,
    layer_scale,
    cotangent,
):
    x, cot = feature_map[0], cotangent[0]
    height, width = x.shape[0], x.shape[1]
    core = lax.axis_index("core").astype(jnp.int32)
    yl = lax.axis_index("yl").astype(jnp.int32)
    top, bot = shifted(x, TALL, 0)
    left, right = column_halo(x, top, bot)

    whole = lambda n: [pl.BlockSpec(memory_space=pltpu.VMEM)] * n
    away = lambda v: pltpu.with_memory_space_constraint(v, pltpu.HBM)
    hbm = lambda n: [pl.BlockSpec(memory_space=pltpu.HBM)] * n
    block_out, gconv, mine, send = pl.pallas_call(
        front_kernel,
        out_shape=(
            jax.ShapeDtypeStruct((height, width, D), BF16),
            jax.ShapeDtypeStruct((height, width, D), F32),
            jax.ShapeDtypeStruct((PIECES, ROWS, LANES), BF16),
            jax.ShapeDtypeStruct((PIECES, ROWS, LANES), BF16),
        ),
        in_specs=[pl.BlockSpec(memory_space=pltpu.SMEM)] + hbm(1) + whole(4) + hbm(10),
        out_specs=tuple(whole(2) + hbm(2)),
        scratch_shapes=[
            pltpu.VMEM((height, width, D), BF16),
            pltpu.VMEM((height, width, D), BF16),
            pltpu.VMEM((7, 7, D), F32),
            pltpu.VMEM((D,), F32),
            pltpu.VMEM((D,), F32),
            pltpu.VMEM((D,), F32),
            pltpu.VMEM((D, FF), BF16),
            pltpu.VMEM((FF,), F32),
            pltpu.VMEM((FF, D), BF16),
            pltpu.VMEM((D,), F32),
            pltpu.VMEM((D,), F32),
            pltpu.VMEM((height + 2 * HALO, width + 8, D), F32),
            pltpu.VMEM((height * width, D), F32),
            pltpu.VMEM((2 * height * width, FF), BF16),
            pltpu.VMEM((2 * PIECES, 2 * SHARE, LANES), F32),
            pltpu.VMEM((PIECES, ROWS, LANES), BF16),
            pltpu.VMEM((PIECES, ROWS, LANES), BF16),
            pltpu.SemaphoreType.DMA((25,)),
        ],
        compiler_params=LIMIT,
        name="front",
    )(
        core.reshape(1),
        away(x),
        top,
        bot,
        left,
        right,
        away(cot),
        away(dw_kernel),
        away(dw_bias),
        away(layer_norm_gain),
        away(layer_norm_bias),
        away(w_expand),
        away(b_expand),
        away(w_reduce),
        away(b_reduce),
        away(layer_scale),
    )

    got = lax.ppermute(send, "core", [(0, 1), (1, 0)])
    gtop, gbot = shifted(gconv, TALL, 0)
    gleft, gright = column_halo(gconv, gtop, gbot)

    step = 2
    spec = pl.BlockSpec((step, ROWS, LANES), lambda i: (i, 0, 0))
    free = lambda n: [pl.BlockSpec(memory_space=pl.ANY)] * n
    smem = [pl.BlockSpec(memory_space=pltpu.SMEM)]
    joined = pl.pallas_call(
        join_kernel,
        out_shape=jax.ShapeDtypeStruct((PIECES, ROWS, LANES), BF16),
        grid=(PIECES // step,),
        in_specs=[spec, spec] + free(2),
        out_specs=spec,
        compiler_params=LIMIT,
        name="join",
    )(mine, got, gtop, gbot)
    near = lax.all_to_all(joined, ("zl", "xl", "yl"), 0, 0, tiled=True)
    by_block = pl.pallas_call(
        block_sum_kernel,
        out_shape=jax.ShapeDtypeStruct((PIECES, 4 * FROWS, LANES), BF16),
        in_specs=whole(1) + free(2),
        out_specs=whole(1)[0],
        scratch_shapes=[pltpu.VMEM((ROWS, LANES), F32)],
        compiler_params=LIMIT,
        name="block_sum",
    )(near, gleft, gright)
    middle = lax.all_to_all(by_block, ("zm", "xm", "ym"), 0, 0, tiled=True)
    by_middle = pl.pallas_call(
        middle_sum_kernel,
        out_shape=jax.ShapeDtypeStruct((PIECES, FROWS, LANES), F32),
        in_specs=smem + whole(1),
        out_specs=whole(1)[0],
        compiler_params=LIMIT,
        name="middle_sum",
    )(yl.reshape(1), middle)
    far = lax.all_to_all(by_middle, ("zh", "xh", "yh"), 0, 0, tiled=True)
    grad_in = pl.pallas_call(
        input_grad_kernel,
        out_shape=jax.ShapeDtypeStruct((height, width, D), BF16),
        in_specs=whole(7),
        out_specs=whole(1)[0],
        scratch_shapes=[pltpu.VMEM((height + 2 * HALO, width + 8, D), F32)],
        compiler_params=LIMIT,
        name="input_grad",
    )(gconv, gtop, gbot, gleft, gright, cot, dw_kernel)
    grad_expand, grad_reduce_t, small = pl.pallas_call(
        functools.partial(far_sum_kernel, scale),
        out_shape=(
            jax.ShapeDtypeStruct((DROWS, FROWS), F32),
            jax.ShapeDtypeStruct((DROWS, FROWS), F32),
            jax.ShapeDtypeStruct((2 * PIECES, SHARE, LANES), F32),
        ),
        in_specs=whole(1),
        out_specs=tuple(whole(3)),
        compiler_params=LIMIT,
        name="far_sum",
    )(far)
    small = lax.all_to_all(small, ("zl", "xl", "yl", "core"), 0, 0, tiled=True)
    gker, vectors, gbexp = pl.pallas_call(
        spread_kernel,
        out_shape=(
            jax.ShapeDtypeStruct((7, 7, D), F32),
            jax.ShapeDtypeStruct((5, D), F32),
            jax.ShapeDtypeStruct((FF,), F32),
        ),
        in_specs=whole(1),
        out_specs=tuple(whole(3)),
        compiler_params=LIMIT,
        name="spread",
    )(small)
    return (
        block_out[None],
        grad_in[None],
        grad_expand,
        grad_reduce_t,
        gker,
        vectors,
        gbexp,
    )


def solution(mesh):
    shape = dict(mesh.shape)
    sizes = (shape["rows"] // 4, 2, 2, shape["cols"] // 4, 2, 2, shape["rep"] // 8, 2, 2, 2)
    fine = Mesh(mesh.devices.reshape(sizes), TALL + WIDE + DEEP)
    tile = P(DEEP, TALL, WIDE, None)
    grad = P(DEEP, TALL + WIDE)
    pixels = 16 * 64 * 128
    scale = float(pixels) ** -0.5
    return jax.shard_map(
        functools.partial(per_device, scale),
        mesh=fine,
        in_specs=(tile,) + (P(),) * 9 + (tile,),
        out_specs=(tile, tile, grad, grad, P(), P(), P()),
        check_vma=False,
    )
```

```python
import functools

import jax
import jax.numpy as jnp
from jax import lax
from jax.experimental import pallas as pl
from jax.experimental.pallas import tpu as pltpu
from jax.sharding import Mesh
from jax.sharding import PartitionSpec as P

EPS = 1e-06
INV_ROOT_TWO = 0.7071067811865476
INV_ROOT_TWO_PI = 0.3989422804014327
F32 = jnp.float32
BF16 = jnp.bfloat16
D = 384
FF = 1536
LANES = 128
BLOCKS = D // LANES
HALO = 3
FROWS = 24
DROWS = 24
PIECES = 8
FAR = 64
BIG = BLOCKS * 8 * FROWS
SHARE = 12
ROWS = BIG + 2 * SHARE
TALL = ("zh", "zl")
WIDE = ("xh", "xl")
LIMIT = pltpu.CompilerParams(vmem_limit_bytes=50 * 1024 * 1024)


def matmul(a, b, ca, cb):
    return lax.dot_general(a, b, (((ca,), (cb,)), ((), ())), preferred_element_type=F32)


def fetch_kernel(*refs):
    count = len(refs) // 2
    copies = [
        pltpu.make_async_copy(refs[k], refs[count + k], refs[-1].at[k]) for k in range(count)
    ]
    for c in copies:
        c.start()
    for c in copies:
        c.wait()


def front_kernel(
    core_ref,
    x_ref,
    top_ref,
    bot_ref,
    left_ref,
    right_ref,
    cot_ref,
    dwk_ref,
    dwb_hbm,
    gain_hbm,
    lnb_hbm,
    wexp_ref,
    bexp_hbm,
    wred_ref,
    bred_hbm,
    ls_hbm,
    block_ref,
    gconv_ref,
    send_hbm,
    both,
    stack_ref,
    own_ref,
    dwb_ref,
    gain_ref,
    lnb_ref,
    bexp_ref,
    bred_ref,
    ls_ref,
    xp,
    conv,
    small,
    send_ref,
    sems,
    out_sems,
):
    pairs = (
        (dwb_hbm, dwb_ref),
        (gain_hbm, gain_ref),
        (lnb_hbm, lnb_ref),
        (ls_hbm, ls_ref),
        (bexp_hbm, bexp_ref),
        (bred_hbm, bred_ref),
    )
    copies = [pltpu.make_async_copy(a, b, sems.at[k]) for k, (a, b) in enumerate(pairs)]
    for c in copies:
        c.start()
    height, width = x_ref.shape[0], x_ref.shape[1]
    pixels = height * width
    row = lambda ref: ref[...].reshape(1, -1)
    xp[0:HALO, HALO : HALO + width, :] = top_ref[...].astype(F32)
    xp[HALO + height :, HALO : HALO + width, :] = bot_ref[...].astype(F32)
    xp[:, 0:HALO, :] = left_ref[...].astype(F32)
    xp[:, HALO + width : 2 * HALO + width, :] = right_ref[...].astype(F32)
    small[...] = jnp.zeros_like(small)

    def put(p, l, value):
        at = BLOCKS * (p % 4) + l
        small[p // 4, at : at + 1, :] = value

    xp[HALO : HALO + height, HALO : HALO + width, :] = x_ref[...].astype(F32)
    for l in range(BLOCKS):
        ln = slice(LANES * l, LANES * (l + 1))
        acc = jnp.zeros((height, width, LANES), F32)
        for j in range(7):
            s = xp[:, j : j + width, ln]
            for i in range(7):
                acc = acc + dwk_ref[i, j : j + 1, ln] * s[i : i + height]
        conv[:, ln] = acc.reshape(pixels, LANES)
    for c in copies:
        c.wait()
    flat = conv[...] + row(dwb_ref)
    centered = flat - jnp.mean(flat, axis=-1, keepdims=True)
    inv = lax.rsqrt(jnp.mean(centered * centered, axis=-1, keepdims=True) + EPS)
    xhat = centered * inv
    gain = row(gain_ref)
    normed = (xhat * gain + row(lnb_ref)).astype(BF16)
    grad = cot_ref[...].astype(F32).reshape(pixels, D)
    scaled = grad * row(ls_ref)
    g_branch = scaled.astype(BF16)
    for f in range(4):
        sl = slice(D * f, D * (f + 1))
        pre = matmul(normed, wexp_ref[:, sl], 1, 0) + bexp_ref[sl].reshape(1, D)
        cdf = 0.5 * (1.0 + lax.erf(pre * INV_ROOT_TWO))
        pdf = jnp.exp(-0.5 * pre * pre) * INV_ROOT_TWO_PI
        g_act = matmul(g_branch, wred_ref[sl, :], 1, 1)
        g_pre = g_act * (cdf + pre * pdf)
        both[0:pixels, sl] = g_pre.astype(BF16)
        both[pixels : 2 * pixels, sl] = (pre * cdf).astype(BF16)
        total = jnp.sum(g_pre, axis=0, keepdims=True)
        for l in range(BLOCKS):
            put(54 + f, l, total[:, LANES * l : LANES * (l + 1)])
    branch = matmul(both[pixels : 2 * pixels, :], wred_ref[...], 1, 0) + row(bred_ref)
    block = x_ref[...].astype(F32).reshape(pixels, D) + row(ls_ref) * branch
    block_ref[...] = block.astype(BF16).reshape(height, width, D)
    g_norm = matmul(both[0:pixels, :], wexp_ref[...], 1, 1)
    gx = g_norm * gain
    gconv = inv * (
        gx
        - jnp.mean(gx, axis=-1, keepdims=True)
        - xhat * jnp.mean(gx * xhat, axis=-1, keepdims=True)
    )
    gconv_ref[...] = gconv.reshape(height, width, D)
    sums = (gconv, g_norm * xhat, g_norm, scaled, grad * branch)
    for k, value in enumerate(sums):
        total = jnp.sum(value, axis=0, keepdims=True)
        for l in range(BLOCKS):
            put(49 + k, l, total[:, LANES * l : LANES * (l + 1)])
    for l in range(BLOCKS):
        ln = slice(LANES * l, LANES * (l + 1))
        g3 = gconv_ref[:, :, ln]
        for j in range(7):
            s = xp[:, j : j + width, ln]
            for i in range(7):
                part = jnp.sum(g3 * s[i : i + height], axis=0)
                put(7 * i + j, l, jnp.sum(part, axis=0, keepdims=True))
    value = small[:, 0:SHARE, :]
    small[:, SHARE : 2 * SHARE, :] = value - value.astype(BF16).astype(F32)
    stack_ref[0:pixels, :] = normed
    stack_ref[pixels : 2 * pixels, :] = g_branch
    core = core_ref[0]
    own_ref[...] = small[pl.ds(PIECES * core, PIECES)]
    send_ref[:, BIG:ROWS, :] = small[pl.ds(PIECES * (1 - core), PIECES)].astype(BF16)
    products(1 - core, both, stack_ref[...], send_ref, send_hbm, out_sems)


def products(core, both, stack, out, hbm, sems):
    pixels = stack.shape[0] // 2
    copies = []

    def flush(rows):
        c = pltpu.make_async_copy(out.at[:, rows], hbm.at[:, rows], sems.at[len(copies)])
        c.start()
        copies.append(c)

    flush(slice(BIG, ROWS))
    chan = lax.broadcasted_iota(jnp.int32, (D, D), 0)
    column = lax.broadcasted_iota(jnp.int32, (1, D), 1)
    half = (column >= D // 2).astype(jnp.int32)
    rest = column - (D // 2) * half
    block = (rest * 1366) >> 16
    inside = rest - 2 * DROWS * block
    of_e = inside < DROWS
    base = 4 * DROWS * block + jnp.where(of_e, inside, inside - DROWS)
    pixel = lax.broadcasted_iota(jnp.int32, (2 * pixels, 1), 0)
    keep = jnp.where(pixel < pixels, 1, 0) == jnp.where(of_e, 1, 0)
    lane = lax.broadcasted_iota(jnp.int32, (1, 1, LANES), 2)
    right = []
    for order in range(2):
        turn = half if order == 0 else 1 - half
        pick = (chan == base + 2 * DROWS * turn + DROWS * core).astype(F32).astype(BF16)
        right.append(jnp.where(keep, matmul(stack, pick, 1, 0), 0.0).astype(BF16))
    for low in range(2):
        g = []
        for order in range(2):
            f = low + 2 * order
            part = matmul(both[:, D * f : D * (f + 1)], right[order], 0, 0)
            g.append(part.reshape(2, 4, 2, FROWS, D))
        for zl in range(2):
            for xl in range(2):
                for yl in range(2):
                    one, two = g[yl][zl, :, xl], g[1 - yl][zl, :, xl]
                    pieces = (
                        one[:, :, 0:LANES],
                        jnp.where(
                            lane < LANES // 2,
                            one[:, :, LANES : 2 * LANES],
                            two[:, :, LANES : 2 * LANES],
                        ),
                        two[:, :, 2 * LANES : D],
                    )
                    for l, piece in enumerate(pieces):
                        at = 8 * FROWS * l + 4 * FROWS * low
                        out[4 * zl + 2 * xl + yl, at : at + 4 * FROWS, :] = piece.reshape(
                            4 * FROWS, LANES
                        ).astype(BF16)
        for l in range(BLOCKS):
            at = 8 * FROWS * l + 4 * FROWS * low
            flush(slice(at, at + 4 * FROWS))
    for c in copies:
        c.wait()


def own_kernel(core_ref, both_ref, stack_ref, small_ref, out_hbm, out_ref, sems):
    out_ref[:, BIG:ROWS, :] = small_ref[...].astype(BF16)
    products(core_ref[0], both_ref, stack_ref[...], out_ref, out_hbm, sems)


def join_kernel(mine_ref, got_ref, out_ref):
    big = mine_ref[:, 0:BIG, :].astype(F32) + got_ref[:, 0:BIG, :].astype(F32)
    out_ref[:, 0:BIG, :] = big.astype(BF16)
    both = mine_ref[:, BIG:ROWS, :].astype(F32) + got_ref[:, BIG:ROWS, :].astype(F32)
    value = both[:, 0:SHARE] + both[:, SHARE : 2 * SHARE]
    low = value - value.astype(BF16).astype(F32)
    out_ref[:, BIG:ROWS, :] = jnp.concatenate([value, low], axis=1).astype(BF16)


def block_sum_kernel(yl_ref, got_ref, top_any, bot_any, out_ref, total):
    total[...] = jnp.sum(got_ref[...].astype(F32), axis=0)
    small = total[BIG : BIG + SHARE, :] + total[BIG + SHARE : ROWS, :]
    side = LANES // 2
    folded = jnp.concatenate([small[:, 0:side], small[:, side:]], axis=0)
    gap = jnp.zeros((FROWS, side - 2 * DROWS), F32)
    tail = jnp.concatenate([gap, folded], axis=1)
    for low in range(2):
        for xh in range(4):
            at = 4 * FROWS * low + FROWS * xh
            wide = jnp.concatenate(
                [
                    total[8 * FROWS * l + at : 8 * FROWS * l + at + FROWS, :]
                    for l in range(BLOCKS)
                ],
                axis=1,
            )
            for half in range(2):
                turn = yl_ref[0] if half == 0 else 1 - yl_ref[0]
                zh = low + 2 * turn
                for yh in range(4):
                    start = D // 2 * half + 2 * DROWS * yh
                    piece = jnp.concatenate([wide[:, start : start + 2 * DROWS], tail], axis=1)
                    out_ref[16 * zh + 4 * xh + yh] = piece.astype(BF16)


def far_sum_kernel(scale, got_ref, left_any, right_any, ge_ref, gr_ref, small_ref):
    total = jnp.sum(got_ref[...].astype(F32), axis=0) * scale
    turned = jnp.transpose(total, (1, 0))
    ge_ref[...] = turned[0:DROWS, 0:FROWS]
    gr_ref[...] = turned[DROWS : 2 * DROWS, 0:FROWS]
    side = LANES // 2
    small = jnp.concatenate([total[0:SHARE, side:], total[SHARE:FROWS, side:]], axis=1)
    small_ref[...] = jnp.broadcast_to(small, small_ref.shape)


def spread_kernel(got_ref, gker_ref, vec_ref, gbexp_ref):
    def take(p, l):
        share, at = p // 4, BLOCKS * (p % 4) + l
        return got_ref[2 * (share % PIECES) + share // PIECES, at : at + 1, :]

    for l in range(BLOCKS):
        ln = slice(LANES * l, LANES * (l + 1))
        for i in range(7):
            for j in range(7):
                gker_ref[i, j : j + 1, ln] = take(7 * i + j, l)
        for k in range(5):
            vec_ref[k : k + 1, ln] = take(49 + k, l)
        for f in range(4):
            at = D * f + LANES * l
            gbexp_ref[at : at + LANES] = take(54 + f, l).reshape(LANES)


def input_grad_kernel(g_ref, top_ref, bot_ref, left_ref, right_ref, cot_ref, dwk_ref, out_ref, gp):
    height, width = g_ref.shape[0], g_ref.shape[1]
    gp[HALO : HALO + height, HALO : HALO + width, :] = g_ref[...]
    gp[0:HALO, HALO : HALO + width, :] = top_ref[...].astype(F32)
    gp[HALO + height :, HALO : HALO + width, :] = bot_ref[...].astype(F32)
    gp[:, 0:HALO, :] = left_ref[...].astype(F32)
    gp[:, HALO + width : 2 * HALO + width, :] = right_ref[...].astype(F32)
    for l in range(BLOCKS):
        ln = slice(LANES * l, LANES * (l + 1))
        acc = cot_ref[:, :, ln].astype(F32)
        for j in range(7):
            s = gp[:, 6 - j : 6 - j + width, ln]
            for i in range(7):
                acc = acc + dwk_ref[i, j : j + 1, ln] * s[6 - i : 6 - i + height]
        out_ref[:, :, ln] = acc.astype(BF16)


def shifted(cells, axis, dim):
    count = lax.axis_size(axis)
    size = cells.shape[dim]
    head = lax.slice_in_dim(cells, 0, HALO, axis=dim)
    tail = lax.slice_in_dim(cells, size - HALO, size, axis=dim)
    before = lax.ppermute(tail, axis, [(i, i + 1) for i in range(count - 1)])
    after = lax.ppermute(head, axis, [(i + 1, i) for i in range(count - 1)])
    return before, after


def column_halo(cells, top, bot):
    width = cells.shape[1]
    head = jnp.concatenate([a[:, 0:HALO] for a in (top, cells, bot)], axis=0)
    tail = jnp.concatenate([a[:, width - HALO :] for a in (top, cells, bot)], axis=0)
    count = lax.axis_size(WIDE)
    left = lax.ppermute(tail, WIDE, [(i, i + 1) for i in range(count - 1)])
    right = lax.ppermute(head, WIDE, [(i + 1, i) for i in range(count - 1)])
    return left, right


def per_device(
    scale,
    feature_map,
    dw_kernel,
    dw_bias,
    layer_norm_gain,
    layer_norm_bias,
    w_expand,
    b_expand,
    w_reduce,
    b_reduce,
    layer_scale,
    cotangent,
):
    x, cot = feature_map[0], cotangent[0]
    height, width = x.shape[0], x.shape[1]
    core = lax.axis_index("core").astype(jnp.int32)
    yl = lax.axis_index("yl").astype(jnp.int32)
    top, bot = shifted(x, TALL, 0)
    left, right = column_halo(x, top, bot)

    whole = lambda n: [pl.BlockSpec(memory_space=pltpu.VMEM)] * n
    away = lambda v: pltpu.with_memory_space_constraint(v, pltpu.HBM)
    hbm = lambda n: [pl.BlockSpec(memory_space=pltpu.HBM)] * n
    fetched = (x, cot, dw_kernel, w_expand, w_reduce)
    x_near, cot_near, dwk_near, wexp_near, wred_near = pl.pallas_call(
        fetch_kernel,
        out_shape=tuple(jax.ShapeDtypeStruct(v.shape, v.dtype) for v in fetched),
        in_specs=hbm(5),
        out_specs=tuple(whole(5)),
        scratch_shapes=[pltpu.SemaphoreType.DMA((5,))],
        compiler_params=LIMIT,
        name="fetch",
    )(*[away(v) for v in fetched])
    smem = [pl.BlockSpec(memory_space=pltpu.SMEM)]
    pixels = height * width
    block_out, gconv, send, both, stack, own = pl.pallas_call(
        front_kernel,
        out_shape=(
            jax.ShapeDtypeStruct((height, width, D), BF16),
            jax.ShapeDtypeStruct((height, width, D), F32),
            jax.ShapeDtypeStruct((PIECES, ROWS, LANES), BF16),
            jax.ShapeDtypeStruct((2 * pixels, FF), BF16),
            jax.ShapeDtypeStruct((2 * pixels, D), BF16),
            jax.ShapeDtypeStruct((PIECES, 2 * SHARE, LANES), F32),
        ),
        in_specs=smem + whole(7) + hbm(3) + whole(1) + hbm(1) + whole(1) + hbm(2),
        out_specs=tuple(whole(2) + hbm(1) + whole(3)),
        scratch_shapes=[
            pltpu.VMEM((D,), F32),
            pltpu.VMEM((D,), F32),
            pltpu.VMEM((D,), F32),
            pltpu.VMEM((FF,), F32),
            pltpu.VMEM((D,), F32),
            pltpu.VMEM((D,), F32),
            pltpu.VMEM((height + 2 * HALO, width + 8, D), F32),
            pltpu.VMEM((pixels, D), F32),
            pltpu.VMEM((2 * PIECES, 2 * SHARE, LANES), F32),
            pltpu.VMEM((PIECES, ROWS, LANES), BF16),
            pltpu.SemaphoreType.DMA((6,)),
            pltpu.SemaphoreType.DMA((7,)),
        ],
        compiler_params=LIMIT,
        name="front",
    )(
        core.reshape(1),
        x_near,
        top,
        bot,
        left,
        right,
        cot_near,
        dwk_near,
        away(dw_bias),
        away(layer_norm_gain),
        away(layer_norm_bias),
        wexp_near,
        away(b_expand),
        wred_near,
        away(b_reduce),
        away(layer_scale),
    )

    got = lax.ppermute(send, "core", [(0, 1), (1, 0)])
    mine = pl.pallas_call(
        own_kernel,
        out_shape=jax.ShapeDtypeStruct((PIECES, ROWS, LANES), BF16),
        in_specs=smem + whole(3),
        out_specs=hbm(1)[0],
        scratch_shapes=[
            pltpu.VMEM((PIECES, ROWS, LANES), BF16),
            pltpu.SemaphoreType.DMA((7,)),
        ],
        compiler_params=LIMIT,
        name="own",
    )(core.reshape(1), both, stack, own)
    edges = gconv.astype(BF16)
    gtop, gbot = shifted(edges, TALL, 0)
    gleft, gright = column_halo(edges, gtop, gbot)

    step = 2
    spec = pl.BlockSpec((step, ROWS, LANES), lambda i: (i, 0, 0))
    free = lambda n: [pl.BlockSpec(memory_space=pl.ANY)] * n
    joined = pl.pallas_call(
        join_kernel,
        out_shape=jax.ShapeDtypeStruct((PIECES, ROWS, LANES), BF16),
        grid=(PIECES // step,),
        in_specs=[spec, spec],
        out_specs=spec,
        compiler_params=LIMIT,
        name="join",
    )(mine, got)
    near = lax.all_to_all(joined, ("zl", "xl", "yl"), 0, 0, tiled=True)
    by_block = pl.pallas_call(
        block_sum_kernel,
        out_shape=jax.ShapeDtypeStruct((FAR, FROWS, LANES), BF16),
        in_specs=smem + whole(1) + free(2),
        out_specs=whole(1)[0],
        scratch_shapes=[pltpu.VMEM((ROWS, LANES), F32)],
        compiler_params=LIMIT,
        name="block_sum",
    )(yl.reshape(1), near, gtop, gbot)
    grad_in = pl.pallas_call(
        input_grad_kernel,
        out_shape=jax.ShapeDtypeStruct((height, width, D), BF16),
        in_specs=whole(7),
        out_specs=whole(1)[0],
        scratch_shapes=[pltpu.VMEM((height + 2 * HALO, width + 8, D), F32)],
        compiler_params=LIMIT,
        name="input_grad",
    )(gconv, gtop, gbot, gleft, gright, cot_near, dwk_near)
    by_block = lax.all_to_all(by_block, ("zh", "xh", "yh"), 0, 0, tiled=True)
    grad_expand, grad_reduce_t, small = pl.pallas_call(
        functools.partial(far_sum_kernel, scale),
        out_shape=(
            jax.ShapeDtypeStruct((DROWS, FROWS), F32),
            jax.ShapeDtypeStruct((DROWS, FROWS), F32),
            jax.ShapeDtypeStruct((2 * PIECES, SHARE, LANES), F32),
        ),
        in_specs=whole(1) + free(2),
        out_specs=tuple(whole(3)),
        compiler_params=LIMIT,
        name="far_sum",
    )(by_block, gleft, gright)
    small = lax.all_to_all(small, ("zl", "xl", "yl", "core"), 0, 0, tiled=True)
    gker, vectors, gbexp = pl.pallas_call(
        spread_kernel,
        out_shape=(
            jax.ShapeDtypeStruct((7, 7, D), F32),
            jax.ShapeDtypeStruct((5, D), F32),
            jax.ShapeDtypeStruct((FF,), F32),
        ),
        in_specs=whole(1),
        out_specs=tuple(whole(3)),
        compiler_params=LIMIT,
        name="spread",
    )(small)
    return (
        block_out[None],
        grad_in[None],
        grad_expand,
        grad_reduce_t,
        gker,
        vectors,
        gbexp,
    )


def solution(mesh):
    shape = dict(mesh.shape)
    sizes = (shape["rows"] // 2, 2, shape["cols"] // 2, 2, shape["rep"] // 4, 2, 2)
    fine = Mesh(mesh.devices.reshape(sizes), TALL + WIDE + ("yh", "yl", "core"))
    tile = P(("yh", "yl", "core"), TALL, WIDE, None)
    grad = P(("yh", "yl", "core"), TALL + WIDE)
    pixels = 16 * 64 * 128
    scale = float(pixels) ** -0.5
    return jax.shard_map(
        functools.partial(per_device, scale),
        mesh=fine,
        in_specs=(tile,) + (P(),) * 9 + (tile,),
        out_specs=(tile, tile, grad, grad, P(), P(), P()),
        check_vma=False,
    )
```

```python
import functools

import jax
import jax.numpy as jnp
from jax import lax
from jax.experimental import pallas as pl
from jax.experimental.pallas import tpu as pltpu
from jax.sharding import Mesh
from jax.sharding import PartitionSpec as P

EPS = 1e-06
INV_ROOT_TWO = 0.7071067811865476
INV_ROOT_TWO_PI = 0.3989422804014327
F32 = jnp.float32
BF16 = jnp.bfloat16
D = 384
FF = 1536
LANES = 128
BLOCKS = D // LANES
HALO = 3
FROWS = 24
DROWS = 24
PIECES = 8
FAR = 64
BIG = BLOCKS * 8 * FROWS
SHARE = 12
ROWS = BIG + 2 * SHARE
TALL = ("zh", "zl")
WIDE = ("xh", "xl")
LIMIT = pltpu.CompilerParams(vmem_limit_bytes=30 * 1024 * 1024)


def matmul(a, b, ca, cb):
    return lax.dot_general(a, b, (((ca,), (cb,)), ((), ())), preferred_element_type=F32)


def fetch_kernel(*refs):
    count = len(refs) // 2
    copies = [
        pltpu.make_async_copy(refs[k], refs[count + k], refs[-1].at[k]) for k in range(count)
    ]
    for c in copies:
        c.start()
    for c in copies:
        c.wait()


def front_kernel(
    core_ref,
    x_ref,
    top_ref,
    bot_ref,
    left_ref,
    right_ref,
    cot_ref,
    dwk_ref,
    dwb_hbm,
    gain_hbm,
    lnb_hbm,
    wexp_ref,
    bexp_hbm,
    wred_ref,
    bred_hbm,
    ls_hbm,
    block_ref,
    gconv_ref,
    send_hbm,
    both,
    stack_ref,
    own_ref,
    dwb_ref,
    gain_ref,
    lnb_ref,
    bexp_ref,
    bred_ref,
    ls_ref,
    xp,
    conv,
    small,
    send_ref,
    sems,
    out_sems,
):
    pairs = (
        (dwb_hbm, dwb_ref),
        (gain_hbm, gain_ref),
        (lnb_hbm, lnb_ref),
        (ls_hbm, ls_ref),
        (bexp_hbm, bexp_ref),
        (bred_hbm, bred_ref),
    )
    copies = [pltpu.make_async_copy(a, b, sems.at[k]) for k, (a, b) in enumerate(pairs)]
    for c in copies:
        c.start()
    height, width = x_ref.shape[0], x_ref.shape[1]
    pixels = height * width
    row = lambda ref: ref[...].reshape(1, -1)
    xp[0:HALO, HALO : HALO + width, :] = top_ref[...].astype(F32)
    xp[HALO + height :, HALO : HALO + width, :] = bot_ref[...].astype(F32)
    xp[:, 0:HALO, :] = left_ref[...].astype(F32)
    xp[:, HALO + width : 2 * HALO + width, :] = right_ref[...].astype(F32)
    small[...] = jnp.zeros_like(small)

    def put(p, l, value):
        at = BLOCKS * (p % 4) + l
        small[p // 4, at : at + 1, :] = value

    xp[HALO : HALO + height, HALO : HALO + width, :] = x_ref[...].astype(F32)
    for l in range(BLOCKS):
        ln = slice(LANES * l, LANES * (l + 1))
        acc = jnp.zeros((height, width, LANES), F32)
        for j in range(7):
            s = xp[:, j : j + width, ln]
            for i in range(7):
                acc = acc + dwk_ref[i, j : j + 1, ln] * s[i : i + height]
        conv[:, ln] = acc.reshape(pixels, LANES)
    for c in copies:
        c.wait()
    flat = conv[...] + row(dwb_ref)
    centered = flat - jnp.mean(flat, axis=-1, keepdims=True)
    inv = lax.rsqrt(jnp.mean(centered * centered, axis=-1, keepdims=True) + EPS)
    xhat = centered * inv
    gain = row(gain_ref)
    normed = (xhat * gain + row(lnb_ref)).astype(BF16)
    grad = cot_ref[...].astype(F32).reshape(pixels, D)
    scaled = grad * row(ls_ref)
    g_branch = scaled.astype(BF16)
    for f in range(4):
        sl = slice(D * f, D * (f + 1))
        pre = matmul(normed, wexp_ref[:, sl], 1, 0) + bexp_ref[sl].reshape(1, D)
        cdf = 0.5 * (1.0 + lax.erf(pre * INV_ROOT_TWO))
        pdf = jnp.exp(-0.5 * pre * pre) * INV_ROOT_TWO_PI
        g_act = matmul(g_branch, wred_ref[sl, :], 1, 1)
        g_pre = g_act * (cdf + pre * pdf)
        both[0:pixels, sl] = g_pre.astype(BF16)
        both[pixels : 2 * pixels, sl] = (pre * cdf).astype(BF16)
        total = jnp.sum(g_pre, axis=0, keepdims=True)
        for l in range(BLOCKS):
            put(54 + f, l, total[:, LANES * l : LANES * (l + 1)])
    branch = matmul(both[pixels : 2 * pixels, :], wred_ref[...], 1, 0) + row(bred_ref)
    block = x_ref[...].astype(F32).reshape(pixels, D) + row(ls_ref) * branch
    block_ref[...] = block.astype(BF16).reshape(height, width, D)
    g_norm = matmul(both[0:pixels, :], wexp_ref[...], 1, 1)
    gx = g_norm * gain
    gconv = inv * (
        gx
        - jnp.mean(gx, axis=-1, keepdims=True)
        - xhat * jnp.mean(gx * xhat, axis=-1, keepdims=True)
    )
    gconv_ref[...] = gconv.reshape(height, width, D)
    sums = (gconv, g_norm * xhat, g_norm, scaled, grad * branch)
    for k, value in enumerate(sums):
        total = jnp.sum(value, axis=0, keepdims=True)
        for l in range(BLOCKS):
            put(49 + k, l, total[:, LANES * l : LANES * (l + 1)])
    for l in range(BLOCKS):
        ln = slice(LANES * l, LANES * (l + 1))
        g3 = gconv_ref[:, :, ln]
        for j in range(7):
            s = xp[:, j : j + width, ln]
            for i in range(7):
                part = jnp.sum(g3 * s[i : i + height], axis=0)
                put(7 * i + j, l, jnp.sum(part, axis=0, keepdims=True))
    value = small[:, 0:SHARE, :]
    small[:, SHARE : 2 * SHARE, :] = value - value.astype(BF16).astype(F32)
    stack_ref[0:pixels, :] = normed
    stack_ref[pixels : 2 * pixels, :] = g_branch
    core = core_ref[0]
    own_ref[...] = small[pl.ds(PIECES * core, PIECES)]
    send_ref[:, BIG:ROWS, :] = small[pl.ds(PIECES * (1 - core), PIECES)].astype(BF16)
    products(1 - core, both, stack_ref[...], send_ref, send_hbm, out_sems)


def products(core, both, stack, out, hbm, sems):
    pixels = stack.shape[0] // 2
    copies = []

    def flush(rows):
        c = pltpu.make_async_copy(out.at[:, rows], hbm.at[:, rows], sems.at[len(copies)])
        c.start()
        copies.append(c)

    flush(slice(BIG, ROWS))
    chan = lax.broadcasted_iota(jnp.int32, (D, D), 0)
    column = lax.broadcasted_iota(jnp.int32, (1, D), 1)
    half = (column >= D // 2).astype(jnp.int32)
    rest = column - (D // 2) * half
    block = (rest * 1366) >> 16
    inside = rest - 2 * DROWS * block
    of_e = inside < DROWS
    base = 4 * DROWS * block + jnp.where(of_e, inside, inside - DROWS)
    pixel = lax.broadcasted_iota(jnp.int32, (2 * pixels, 1), 0)
    keep = jnp.where(pixel < pixels, 1, 0) == jnp.where(of_e, 1, 0)
    lane = lax.broadcasted_iota(jnp.int32, (1, 1, LANES), 2)
    right = []
    for order in range(2):
        turn = half if order == 0 else 1 - half
        pick = (chan == base + 2 * DROWS * turn + DROWS * core).astype(F32).astype(BF16)
        right.append(jnp.where(keep, matmul(stack, pick, 1, 0), 0.0).astype(BF16))
    for low in range(2):
        g = []
        for order in range(2):
            f = low + 2 * order
            part = matmul(both[:, D * f : D * (f + 1)], right[order], 0, 0)
            g.append(part.reshape(2, 4, 2, FROWS, D))
        for zl in range(2):
            for xl in range(2):
                for yl in range(2):
                    one, two = g[yl][zl, :, xl], g[1 - yl][zl, :, xl]
                    pieces = (
                        one[:, :, 0:LANES],
                        jnp.where(
                            lane < LANES // 2,
                            one[:, :, LANES : 2 * LANES],
                            two[:, :, LANES : 2 * LANES],
                        ),
                        two[:, :, 2 * LANES : D],
                    )
                    for l, piece in enumerate(pieces):
                        at = 8 * FROWS * l + 4 * FROWS * low
                        out[4 * zl + 2 * xl + yl, at : at + 4 * FROWS, :] = piece.reshape(
                            4 * FROWS, LANES
                        ).astype(BF16)
        for l in range(BLOCKS):
            at = 8 * FROWS * l + 4 * FROWS * low
            flush(slice(at, at + 4 * FROWS))
    for c in copies:
        c.wait()


def own_kernel(core_ref, both_ref, stack_ref, small_ref, out_hbm, out_ref, sems):
    out_ref[:, BIG:ROWS, :] = small_ref[...].astype(BF16)
    products(core_ref[0], both_ref, stack_ref[...], out_ref, out_hbm, sems)


def join_kernel(mine_ref, got_ref, out_hbm, out_ref, sems):
    both = mine_ref[:, BIG:ROWS, :].astype(F32) + got_ref[:, BIG:ROWS, :].astype(F32)
    value = both[:, 0:SHARE] + both[:, SHARE : 2 * SHARE]
    low = value - value.astype(BF16).astype(F32)
    out_ref[:, BIG:ROWS, :] = jnp.concatenate([value, low], axis=1).astype(BF16)
    copies = []
    for k in range(PIECES):
        big = mine_ref[k, 0:BIG, :].astype(F32) + got_ref[k, 0:BIG, :].astype(F32)
        out_ref[k, 0:BIG, :] = big.astype(BF16)
        c = pltpu.make_async_copy(out_ref.at[k], out_hbm.at[k], sems.at[k])
        c.start()
        copies.append(c)
    for c in copies:
        c.wait()


def block_sum_kernel(yl_ref, got_ref, top_any, bot_any, out_ref, total):
    total[...] = jnp.sum(got_ref[...].astype(F32), axis=0)
    small = total[BIG : BIG + SHARE, :] + total[BIG + SHARE : ROWS, :]
    side = LANES // 2
    folded = jnp.concatenate([small[:, 0:side], small[:, side:]], axis=0)
    gap = jnp.zeros((FROWS, side - 2 * DROWS), F32)
    tail = jnp.concatenate([gap, folded], axis=1)
    for low in range(2):
        for xh in range(4):
            at = 4 * FROWS * low + FROWS * xh
            wide = jnp.concatenate(
                [
                    total[8 * FROWS * l + at : 8 * FROWS * l + at + FROWS, :]
                    for l in range(BLOCKS)
                ],
                axis=1,
            )
            for half in range(2):
                turn = yl_ref[0] if half == 0 else 1 - yl_ref[0]
                zh = low + 2 * turn
                for yh in range(4):
                    start = D // 2 * half + 2 * DROWS * yh
                    piece = jnp.concatenate([wide[:, start : start + 2 * DROWS], tail], axis=1)
                    out_ref[16 * zh + 4 * xh + yh] = piece.astype(BF16)


def far_sum_kernel(scale, got_ref, left_any, right_any, ge_ref, gr_ref, small_ref):
    total = jnp.sum(got_ref[...].astype(F32), axis=0) * scale
    turned = jnp.transpose(total, (1, 0))
    ge_ref[...] = turned[0:DROWS, 0:FROWS]
    gr_ref[...] = turned[DROWS : 2 * DROWS, 0:FROWS]
    side = LANES // 2
    small = jnp.concatenate([total[0:SHARE, side:], total[SHARE:FROWS, side:]], axis=1)
    small_ref[...] = jnp.broadcast_to(small, small_ref.shape)


def spread_kernel(got_ref, gker_ref, vec_ref, gbexp_ref):
    def take(p, l):
        share, at = p // 4, BLOCKS * (p % 4) + l
        return got_ref[2 * (share % PIECES) + share // PIECES, at : at + 1, :]

    for l in range(BLOCKS):
        ln = slice(LANES * l, LANES * (l + 1))
        for i in range(7):
            for j in range(7):
                gker_ref[i, j : j + 1, ln] = take(7 * i + j, l)
        for k in range(5):
            vec_ref[k : k + 1, ln] = take(49 + k, l)
        for f in range(4):
            at = D * f + LANES * l
            gbexp_ref[at : at + LANES] = take(54 + f, l).reshape(LANES)


def input_grad_kernel(g_ref, top_ref, bot_ref, left_ref, right_ref, cot_ref, dwk_ref, out_ref, gp):
    height, width = g_ref.shape[0], g_ref.shape[1]
    gp[HALO : HALO + height, HALO : HALO + width, :] = g_ref[...]
    gp[0:HALO, HALO : HALO + width, :] = top_ref[...].astype(F32)
    gp[HALO + height :, HALO : HALO + width, :] = bot_ref[...].astype(F32)
    gp[:, 0:HALO, :] = left_ref[...].astype(F32)
    gp[:, HALO + width : 2 * HALO + width, :] = right_ref[...].astype(F32)
    for l in range(BLOCKS):
        ln = slice(LANES * l, LANES * (l + 1))
        acc = cot_ref[:, :, ln].astype(F32)
        for j in range(7):
            s = gp[:, 6 - j : 6 - j + width, ln]
            for i in range(7):
                acc = acc + dwk_ref[i, j : j + 1, ln] * s[6 - i : 6 - i + height]
        out_ref[:, :, ln] = acc.astype(BF16)


def shifted(cells, axis, dim):
    count = lax.axis_size(axis)
    size = cells.shape[dim]
    head = lax.slice_in_dim(cells, 0, HALO, axis=dim)
    tail = lax.slice_in_dim(cells, size - HALO, size, axis=dim)
    before = lax.ppermute(tail, axis, [(i, i + 1) for i in range(count - 1)])
    after = lax.ppermute(head, axis, [(i + 1, i) for i in range(count - 1)])
    return before, after


def column_halo(cells, top, bot):
    width = cells.shape[1]
    head = jnp.concatenate([a[:, 0:HALO] for a in (top, cells, bot)], axis=0)
    tail = jnp.concatenate([a[:, width - HALO :] for a in (top, cells, bot)], axis=0)
    count = lax.axis_size(WIDE)
    left = lax.ppermute(tail, WIDE, [(i, i + 1) for i in range(count - 1)])
    right = lax.ppermute(head, WIDE, [(i + 1, i) for i in range(count - 1)])
    return left, right


def per_device(
    scale,
    feature_map,
    dw_kernel,
    dw_bias,
    layer_norm_gain,
    layer_norm_bias,
    w_expand,
    b_expand,
    w_reduce,
    b_reduce,
    layer_scale,
    cotangent,
):
    x, cot = feature_map[0], cotangent[0]
    height, width = x.shape[0], x.shape[1]
    core = lax.axis_index("core").astype(jnp.int32)
    yl = lax.axis_index("yl").astype(jnp.int32)
    top, bot = shifted(x, TALL, 0)

    whole = lambda n: [pl.BlockSpec(memory_space=pltpu.VMEM)] * n
    away = lambda v: pltpu.with_memory_space_constraint(v, pltpu.HBM)
    hbm = lambda n: [pl.BlockSpec(memory_space=pltpu.HBM)] * n
    fetched = (x, cot, dw_kernel, w_expand, w_reduce)
    x_near, cot_near, dwk_near, wexp_near, wred_near = pl.pallas_call(
        fetch_kernel,
        out_shape=tuple(jax.ShapeDtypeStruct(v.shape, v.dtype) for v in fetched),
        in_specs=hbm(5),
        out_specs=tuple(whole(5)),
        scratch_shapes=[pltpu.SemaphoreType.DMA((5,))],
        compiler_params=LIMIT,
        name="fetch",
    )(*[away(v) for v in fetched])
    left, right = column_halo(x_near, top, bot)
    smem = [pl.BlockSpec(memory_space=pltpu.SMEM)]
    pixels = height * width
    block_out, gconv, send, both, stack, own = pl.pallas_call(
        front_kernel,
        out_shape=(
            jax.ShapeDtypeStruct((height, width, D), BF16),
            jax.ShapeDtypeStruct((height, width, D), F32),
            jax.ShapeDtypeStruct((PIECES, ROWS, LANES), BF16),
            jax.ShapeDtypeStruct((2 * pixels, FF), BF16),
            jax.ShapeDtypeStruct((2 * pixels, D), BF16),
            jax.ShapeDtypeStruct((PIECES, 2 * SHARE, LANES), F32),
        ),
        in_specs=smem + whole(7) + hbm(3) + whole(1) + hbm(1) + whole(1) + hbm(2),
        out_specs=tuple(whole(2) + hbm(1) + whole(3)),
        scratch_shapes=[
            pltpu.VMEM((D,), F32),
            pltpu.VMEM((D,), F32),
            pltpu.VMEM((D,), F32),
            pltpu.VMEM((FF,), F32),
            pltpu.VMEM((D,), F32),
            pltpu.VMEM((D,), F32),
            pltpu.VMEM((height + 2 * HALO, width + 8, D), F32),
            pltpu.VMEM((pixels, D), F32),
            pltpu.VMEM((2 * PIECES, 2 * SHARE, LANES), F32),
            pltpu.VMEM((PIECES, ROWS, LANES), BF16),
            pltpu.SemaphoreType.DMA((6,)),
            pltpu.SemaphoreType.DMA((7,)),
        ],
        compiler_params=LIMIT,
        name="front",
    )(
        core.reshape(1),
        x_near,
        top,
        bot,
        left,
        right,
        cot_near,
        dwk_near,
        away(dw_bias),
        away(layer_norm_gain),
        away(layer_norm_bias),
        wexp_near,
        away(b_expand),
        wred_near,
        away(b_reduce),
        away(layer_scale),
    )

    got = lax.ppermute(send, "core", [(0, 1), (1, 0)])
    mine = pl.pallas_call(
        own_kernel,
        out_shape=jax.ShapeDtypeStruct((PIECES, ROWS, LANES), BF16),
        in_specs=smem + whole(3),
        out_specs=hbm(1)[0],
        scratch_shapes=[
            pltpu.VMEM((PIECES, ROWS, LANES), BF16),
            pltpu.SemaphoreType.DMA((7,)),
        ],
        compiler_params=LIMIT,
        name="own",
    )(core.reshape(1), both, stack, own)
    edges = gconv.astype(BF16)
    gtop, gbot = shifted(edges, TALL, 0)
    gleft, gright = column_halo(edges, gtop, gbot)

    free = lambda n: [pl.BlockSpec(memory_space=pl.ANY)] * n
    joined = pl.pallas_call(
        join_kernel,
        out_shape=jax.ShapeDtypeStruct((PIECES, ROWS, LANES), BF16),
        in_specs=whole(2),
        out_specs=hbm(1)[0],
        scratch_shapes=[
            pltpu.VMEM((PIECES, ROWS, LANES), BF16),
            pltpu.SemaphoreType.DMA((PIECES,)),
        ],
        compiler_params=LIMIT,
        name="join",
    )(mine, got)
    near = lax.all_to_all(joined, ("zl", "xl", "yl"), 0, 0, tiled=True)
    by_block = pl.pallas_call(
        block_sum_kernel,
        out_shape=jax.ShapeDtypeStruct((FAR, FROWS, LANES), BF16),
        in_specs=smem + whole(1) + free(2),
        out_specs=whole(1)[0],
        scratch_shapes=[pltpu.VMEM((ROWS, LANES), F32)],
        compiler_params=LIMIT,
        name="block_sum",
    )(yl.reshape(1), near, gtop, gbot)
    grad_in = pl.pallas_call(
        input_grad_kernel,
        out_shape=jax.ShapeDtypeStruct((height, width, D), BF16),
        in_specs=whole(7),
        out_specs=whole(1)[0],
        scratch_shapes=[pltpu.VMEM((height + 2 * HALO, width + 8, D), F32)],
        compiler_params=LIMIT,
        name="input_grad",
    )(gconv, gtop, gbot, gleft, gright, cot_near, dwk_near)
    by_block = lax.all_to_all(by_block, ("zh", "xh", "yh"), 0, 0, tiled=True)
    grad_expand, grad_reduce_t, small = pl.pallas_call(
        functools.partial(far_sum_kernel, scale),
        out_shape=(
            jax.ShapeDtypeStruct((DROWS, FROWS), F32),
            jax.ShapeDtypeStruct((DROWS, FROWS), F32),
            jax.ShapeDtypeStruct((2 * PIECES, SHARE, LANES), F32),
        ),
        in_specs=whole(1) + free(2),
        out_specs=tuple(whole(3)),
        compiler_params=LIMIT,
        name="far_sum",
    )(by_block, gleft, gright)
    small = lax.all_to_all(small, ("zl", "xl", "yl", "core"), 0, 0, tiled=True)
    gker, vectors, gbexp = pl.pallas_call(
        spread_kernel,
        out_shape=(
            jax.ShapeDtypeStruct((7, 7, D), F32),
            jax.ShapeDtypeStruct((5, D), F32),
            jax.ShapeDtypeStruct((FF,), F32),
        ),
        in_specs=whole(1),
        out_specs=tuple(whole(3)),
        compiler_params=LIMIT,
        name="spread",
    )(small)
    return (
        block_out[None],
        grad_in[None],
        grad_expand,
        grad_reduce_t,
        gker,
        vectors,
        gbexp,
    )


def solution(mesh):
    shape = dict(mesh.shape)
    sizes = (shape["rows"] // 2, 2, shape["cols"] // 2, 2, shape["rep"] // 4, 2, 2)
    fine = Mesh(mesh.devices.reshape(sizes), TALL + WIDE + ("yh", "yl", "core"))
    tile = P(("yh", "yl", "core"), TALL, WIDE, None)
    grad = P(("yh", "yl", "core"), TALL + WIDE)
    pixels = 16 * 64 * 128
    scale = float(pixels) ** -0.5
    return jax.shard_map(
        functools.partial(per_device, scale),
        mesh=fine,
        in_specs=(tile,) + (P(),) * 9 + (tile,),
        out_specs=(tile, tile, grad, grad, P(), P(), P()),
        check_vma=False,
    )
```

```python
import functools

import jax
import jax.numpy as jnp
from jax import lax
from jax.experimental import pallas as pl
from jax.experimental.pallas import tpu as pltpu
from jax.sharding import Mesh
from jax.sharding import PartitionSpec as P

EPS = 1e-06
INV_ROOT_TWO = 0.7071067811865476
INV_ROOT_TWO_PI = 0.3989422804014327
F32 = jnp.float32
BF16 = jnp.bfloat16
D = 384
FF = 1536
LANES = 128
BLOCKS = D // LANES
HALO = 3
FROWS = 24
DROWS = 24
PIECES = 8
FAR = 64
BIG = BLOCKS * 8 * FROWS
SHARE = 12
ROWS = BIG + 2 * SHARE
TALL = ("zh", "zl")
WIDE = ("xh", "xl")
LIMIT = pltpu.CompilerParams(vmem_limit_bytes=30 * 1024 * 1024)


def matmul(a, b, ca, cb):
    return lax.dot_general(a, b, (((ca,), (cb,)), ((), ())), preferred_element_type=F32)


def fetch_kernel(*refs):
    count = len(refs) // 2
    copies = [
        pltpu.make_async_copy(refs[k], refs[count + k], refs[-1].at[k]) for k in range(count)
    ]
    for c in copies:
        c.start()
    for c in copies:
        c.wait()


def front_kernel(
    core_ref,
    x_ref,
    top_ref,
    bot_ref,
    left_ref,
    right_ref,
    cot_ref,
    dwk_ref,
    dwb_ref,
    gain_ref,
    lnb_ref,
    wexp_ref,
    bexp_ref,
    wred_ref,
    bred_ref,
    ls_ref,
    block_ref,
    gconv_ref,
    send_hbm,
    both,
    stack_ref,
    own_ref,
    xp,
    conv,
    small,
    send_ref,
    bias_ref,
    out_sems,
):
    first = pltpu.make_async_copy(dwb_ref, bias_ref, out_sems.at[6])
    first.start()
    height, width = x_ref.shape[0], x_ref.shape[1]
    pixels = height * width
    row = lambda ref: ref[...].reshape(1, -1)
    xp[0:HALO, HALO : HALO + width, :] = top_ref[...].astype(F32)
    xp[HALO + height :, HALO : HALO + width, :] = bot_ref[...].astype(F32)
    xp[:, 0:HALO, :] = left_ref[...].astype(F32)
    xp[:, HALO + width : 2 * HALO + width, :] = right_ref[...].astype(F32)
    small[...] = jnp.zeros_like(small)

    def put(p, l, value):
        at = BLOCKS * (p % 4) + l
        small[p // 4, at : at + 1, :] = value

    xp[HALO : HALO + height, HALO : HALO + width, :] = x_ref[...].astype(F32)
    for l in range(BLOCKS):
        ln = slice(LANES * l, LANES * (l + 1))
        acc = jnp.zeros((height, width, LANES), F32)
        for j in range(7):
            s = xp[:, j : j + width, ln]
            for i in range(7):
                acc = acc + dwk_ref[i, j : j + 1, ln] * s[i : i + height]
        conv[:, ln] = acc.reshape(pixels, LANES)
    first.wait()
    flat = conv[...] + row(bias_ref)
    centered = flat - jnp.mean(flat, axis=-1, keepdims=True)
    inv = lax.rsqrt(jnp.mean(centered * centered, axis=-1, keepdims=True) + EPS)
    xhat = centered * inv
    gain = row(gain_ref)
    normed = (xhat * gain + row(lnb_ref)).astype(BF16)
    grad = cot_ref[...].astype(F32).reshape(pixels, D)
    scaled = grad * row(ls_ref)
    g_branch = scaled.astype(BF16)
    for f in range(4):
        sl = slice(D * f, D * (f + 1))
        pre = matmul(normed, wexp_ref[:, sl], 1, 0) + bexp_ref[sl].reshape(1, D)
        cdf = 0.5 * (1.0 + lax.erf(pre * INV_ROOT_TWO))
        pdf = jnp.exp(-0.5 * pre * pre) * INV_ROOT_TWO_PI
        g_act = matmul(g_branch, wred_ref[sl, :], 1, 1)
        g_pre = g_act * (cdf + pre * pdf)
        both[0:pixels, sl] = g_pre.astype(BF16)
        both[pixels : 2 * pixels, sl] = (pre * cdf).astype(BF16)
        total = jnp.sum(g_pre, axis=0, keepdims=True)
        for l in range(BLOCKS):
            put(54 + f, l, total[:, LANES * l : LANES * (l + 1)])
    stack_ref[0:pixels, :] = normed
    stack_ref[pixels : 2 * pixels, :] = g_branch
    outputs = products(1 - core_ref[0], both, stack_ref[...], send_ref, send_hbm, out_sems)
    branch = matmul(both[pixels : 2 * pixels, :], wred_ref[...], 1, 0) + row(bred_ref)
    block = x_ref[...].astype(F32).reshape(pixels, D) + row(ls_ref) * branch
    block_ref[...] = block.astype(BF16).reshape(height, width, D)
    g_norm = matmul(both[0:pixels, :], wexp_ref[...], 1, 1)
    gx = g_norm * gain
    gconv = inv * (
        gx
        - jnp.mean(gx, axis=-1, keepdims=True)
        - xhat * jnp.mean(gx * xhat, axis=-1, keepdims=True)
    )
    gconv_ref[...] = gconv.reshape(height, width, D)
    sums = (gconv, g_norm * xhat, g_norm, scaled, grad * branch)
    for k, value in enumerate(sums):
        total = jnp.sum(value, axis=0, keepdims=True)
        for l in range(BLOCKS):
            put(49 + k, l, total[:, LANES * l : LANES * (l + 1)])
    for l in range(BLOCKS):
        ln = slice(LANES * l, LANES * (l + 1))
        g3 = gconv_ref[:, :, ln]
        for j in range(7):
            s = xp[:, j : j + width, ln]
            for i in range(7):
                part = jnp.sum(g3 * s[i : i + height], axis=0)
                put(7 * i + j, l, jnp.sum(part, axis=0, keepdims=True))
    value = small[:, 0:SHARE, :]
    small[:, SHARE : 2 * SHARE, :] = value - value.astype(BF16).astype(F32)
    core = core_ref[0]
    own_ref[...] = small[pl.ds(PIECES * core, PIECES)]
    send_ref[:, BIG:ROWS, :] = small[pl.ds(PIECES * (1 - core), PIECES)].astype(BF16)
    rows = slice(BIG, ROWS)
    c = pltpu.make_async_copy(send_ref.at[:, rows], send_hbm.at[:, rows], out_sems.at[6])
    c.start()
    for c in outputs + [c]:
        c.wait()


def products(core, both, stack, out, hbm, sems):
    pixels = stack.shape[0] // 2
    copies = []

    def flush(rows):
        c = pltpu.make_async_copy(out.at[:, rows], hbm.at[:, rows], sems.at[len(copies)])
        c.start()
        copies.append(c)

    chan = lax.broadcasted_iota(jnp.int32, (D, D), 0)
    column = lax.broadcasted_iota(jnp.int32, (1, D), 1)
    half = (column >= D // 2).astype(jnp.int32)
    rest = column - (D // 2) * half
    block = (rest * 1366) >> 16
    inside = rest - 2 * DROWS * block
    of_e = inside < DROWS
    base = 4 * DROWS * block + jnp.where(of_e, inside, inside - DROWS)
    pixel = lax.broadcasted_iota(jnp.int32, (2 * pixels, 1), 0)
    keep = jnp.where(pixel < pixels, 1, 0) == jnp.where(of_e, 1, 0)
    lane = lax.broadcasted_iota(jnp.int32, (1, 1, LANES), 2)
    right = []
    for order in range(2):
        turn = half if order == 0 else 1 - half
        pick = (chan == base + 2 * DROWS * turn + DROWS * core).astype(F32).astype(BF16)
        right.append(jnp.where(keep, matmul(stack, pick, 1, 0), 0.0).astype(BF16))
    for low in range(2):
        g = []
        for order in range(2):
            f = low + 2 * order
            part = matmul(both[:, D * f : D * (f + 1)], right[order], 0, 0)
            g.append(part.reshape(2, 4, 2, FROWS, D))
        for zl in range(2):
            for xl in range(2):
                for yl in range(2):
                    one, two = g[yl][zl, :, xl], g[1 - yl][zl, :, xl]
                    pieces = (
                        one[:, :, 0:LANES],
                        jnp.where(
                            lane < LANES // 2,
                            one[:, :, LANES : 2 * LANES],
                            two[:, :, LANES : 2 * LANES],
                        ),
                        two[:, :, 2 * LANES : D],
                    )
                    for l, piece in enumerate(pieces):
                        at = 8 * FROWS * l + 4 * FROWS * low
                        out[4 * zl + 2 * xl + yl, at : at + 4 * FROWS, :] = piece.reshape(
                            4 * FROWS, LANES
                        ).astype(BF16)
        for l in range(BLOCKS):
            at = 8 * FROWS * l + 4 * FROWS * low
            flush(slice(at, at + 4 * FROWS))
    return copies


def own_kernel(core_ref, both_ref, stack_ref, small_ref, out_hbm, out_ref, sems):
    out_ref[:, BIG:ROWS, :] = small_ref[...].astype(BF16)
    rows = slice(BIG, ROWS)
    c = pltpu.make_async_copy(out_ref.at[:, rows], out_hbm.at[:, rows], sems.at[6])
    c.start()
    for c in products(core_ref[0], both_ref, stack_ref[...], out_ref, out_hbm, sems) + [c]:
        c.wait()


def join_kernel(mine_ref, got_ref, out_hbm, out_ref, sems):
    both = mine_ref[:, BIG:ROWS, :].astype(F32) + got_ref[:, BIG:ROWS, :].astype(F32)
    value = both[:, 0:SHARE] + both[:, SHARE : 2 * SHARE]
    low = value - value.astype(BF16).astype(F32)
    out_ref[:, BIG:ROWS, :] = jnp.concatenate([value, low], axis=1).astype(BF16)
    copies = []
    for k in range(PIECES):
        big = mine_ref[k, 0:BIG, :].astype(F32) + got_ref[k, 0:BIG, :].astype(F32)
        out_ref[k, 0:BIG, :] = big.astype(BF16)
        c = pltpu.make_async_copy(out_ref.at[k], out_hbm.at[k], sems.at[k])
        c.start()
        copies.append(c)
    for c in copies:
        c.wait()


def block_sum_kernel(yl_ref, got_ref, top_any, bot_any, out_ref, total):
    total[...] = jnp.sum(got_ref[...].astype(F32), axis=0)
    small = total[BIG : BIG + SHARE, :] + total[BIG + SHARE : ROWS, :]
    side = LANES // 2
    folded = jnp.concatenate([small[:, 0:side], small[:, side:]], axis=0)
    gap = jnp.zeros((FROWS, side - 2 * DROWS), F32)
    tail = jnp.concatenate([gap, folded], axis=1)
    for low in range(2):
        for xh in range(4):
            at = 4 * FROWS * low + FROWS * xh
            wide = jnp.concatenate(
                [
                    total[8 * FROWS * l + at : 8 * FROWS * l + at + FROWS, :]
                    for l in range(BLOCKS)
                ],
                axis=1,
            )
            for half in range(2):
                turn = yl_ref[0] if half == 0 else 1 - yl_ref[0]
                zh = low + 2 * turn
                for yh in range(4):
                    start = D // 2 * half + 2 * DROWS * yh
                    piece = jnp.concatenate([wide[:, start : start + 2 * DROWS], tail], axis=1)
                    out_ref[16 * zh + 4 * xh + yh] = piece.astype(BF16)


def far_sum_kernel(scale, got_ref, left_any, right_any, ge_ref, gr_ref, small_ref):
    total = jnp.sum(got_ref[...].astype(F32), axis=0) * scale
    turned = jnp.transpose(total, (1, 0))
    ge_ref[...] = turned[0:DROWS, 0:FROWS]
    gr_ref[...] = turned[DROWS : 2 * DROWS, 0:FROWS]
    side = LANES // 2
    small = jnp.concatenate([total[0:SHARE, side:], total[SHARE:FROWS, side:]], axis=1)
    small_ref[...] = jnp.broadcast_to(small, small_ref.shape)


def spread_kernel(got_ref, gker_ref, vec_ref, gbexp_ref):
    def take(p, l):
        share, at = p // 4, BLOCKS * (p % 4) + l
        return got_ref[2 * (share % PIECES) + share // PIECES, at : at + 1, :]

    for l in range(BLOCKS):
        ln = slice(LANES * l, LANES * (l + 1))
        for i in range(7):
            for j in range(7):
                gker_ref[i, j : j + 1, ln] = take(7 * i + j, l)
        for k in range(5):
            vec_ref[k : k + 1, ln] = take(49 + k, l)
        for f in range(4):
            at = D * f + LANES * l
            gbexp_ref[at : at + LANES] = take(54 + f, l).reshape(LANES)


def input_grad_kernel(g_ref, top_ref, bot_ref, left_ref, right_ref, cot_ref, dwk_ref, out_ref, gp):
    height, width = g_ref.shape[0], g_ref.shape[1]
    gp[HALO : HALO + height, HALO : HALO + width, :] = g_ref[...]
    gp[0:HALO, HALO : HALO + width, :] = top_ref[...].astype(F32)
    gp[HALO + height :, HALO : HALO + width, :] = bot_ref[...].astype(F32)
    gp[:, 0:HALO, :] = left_ref[...].astype(F32)
    gp[:, HALO + width : 2 * HALO + width, :] = right_ref[...].astype(F32)
    for l in range(BLOCKS):
        ln = slice(LANES * l, LANES * (l + 1))
        acc = cot_ref[:, :, ln].astype(F32)
        for j in range(7):
            s = gp[:, 6 - j : 6 - j + width, ln]
            for i in range(7):
                acc = acc + dwk_ref[i, j : j + 1, ln] * s[6 - i : 6 - i + height]
        out_ref[:, :, ln] = acc.astype(BF16)


def shifted(cells, axis, dim):
    count = lax.axis_size(axis)
    size = cells.shape[dim]
    head = lax.slice_in_dim(cells, 0, HALO, axis=dim)
    tail = lax.slice_in_dim(cells, size - HALO, size, axis=dim)
    before = lax.ppermute(tail, axis, [(i, i + 1) for i in range(count - 1)])
    after = lax.ppermute(head, axis, [(i + 1, i) for i in range(count - 1)])
    return before, after


def column_halo(cells, top, bot):
    width = cells.shape[1]
    head = jnp.concatenate([a[:, 0:HALO] for a in (top, cells, bot)], axis=0)
    tail = jnp.concatenate([a[:, width - HALO :] for a in (top, cells, bot)], axis=0)
    count = lax.axis_size(WIDE)
    left = lax.ppermute(tail, WIDE, [(i, i + 1) for i in range(count - 1)])
    right = lax.ppermute(head, WIDE, [(i + 1, i) for i in range(count - 1)])
    return left, right


def per_device(
    scale,
    feature_map,
    dw_kernel,
    dw_bias,
    layer_norm_gain,
    layer_norm_bias,
    w_expand,
    b_expand,
    w_reduce,
    b_reduce,
    layer_scale,
    cotangent,
):
    x, cot = feature_map[0], cotangent[0]
    height, width = x.shape[0], x.shape[1]
    core = lax.axis_index("core").astype(jnp.int32)
    yl = lax.axis_index("yl").astype(jnp.int32)
    top, bot = shifted(x, TALL, 0)

    whole = lambda n: [pl.BlockSpec(memory_space=pltpu.VMEM)] * n
    away = lambda v: pltpu.with_memory_space_constraint(v, pltpu.HBM)
    hbm = lambda n: [pl.BlockSpec(memory_space=pltpu.HBM)] * n
    fetched = (
        x,
        cot,
        dw_kernel,
        w_expand,
        w_reduce,
        dw_bias,
        layer_norm_gain,
        layer_norm_bias,
        b_expand,
        b_reduce,
        layer_scale,
    )
    x_near, cot_near, dwk_near, wexp_near, wred_near, dwb, gain, lnb, bexp, bred, ls = pl.pallas_call(
        fetch_kernel,
        out_shape=tuple(jax.ShapeDtypeStruct(v.shape, v.dtype) for v in fetched),
        in_specs=hbm(11),
        out_specs=tuple(whole(11)),
        scratch_shapes=[pltpu.SemaphoreType.DMA((11,))],
        compiler_params=LIMIT,
        name="fetch",
    )(*[away(v) for v in fetched])
    left, right = column_halo(x_near, top, bot)
    smem = [pl.BlockSpec(memory_space=pltpu.SMEM)]
    pixels = height * width
    block_out, gconv, send, both, stack, own = pl.pallas_call(
        front_kernel,
        out_shape=(
            jax.ShapeDtypeStruct((height, width, D), BF16),
            jax.ShapeDtypeStruct((height, width, D), F32),
            jax.ShapeDtypeStruct((PIECES, ROWS, LANES), BF16),
            jax.ShapeDtypeStruct((2 * pixels, FF), BF16),
            jax.ShapeDtypeStruct((2 * pixels, D), BF16),
            jax.ShapeDtypeStruct((PIECES, 2 * SHARE, LANES), F32),
        ),
        in_specs=smem + whole(15),
        out_specs=tuple(whole(2) + hbm(1) + whole(3)),
        scratch_shapes=[
            pltpu.VMEM((height + 2 * HALO, width + 8, D), F32),
            pltpu.VMEM((pixels, D), F32),
            pltpu.VMEM((2 * PIECES, 2 * SHARE, LANES), F32),
            pltpu.VMEM((PIECES, ROWS, LANES), BF16),
            pltpu.VMEM((D,), F32),
            pltpu.SemaphoreType.DMA((7,)),
        ],
        compiler_params=LIMIT,
        name="front",
    )(
        core.reshape(1),
        x_near,
        top,
        bot,
        left,
        right,
        cot_near,
        dwk_near,
        dwb,
        gain,
        lnb,
        wexp_near,
        bexp,
        wred_near,
        bred,
        ls,
    )

    got = lax.ppermute(send, "core", [(0, 1), (1, 0)])
    mine = pl.pallas_call(
        own_kernel,
        out_shape=jax.ShapeDtypeStruct((PIECES, ROWS, LANES), BF16),
        in_specs=smem + whole(3),
        out_specs=hbm(1)[0],
        scratch_shapes=[
            pltpu.VMEM((PIECES, ROWS, LANES), BF16),
            pltpu.SemaphoreType.DMA((7,)),
        ],
        compiler_params=LIMIT,
        name="own",
    )(core.reshape(1), both, stack, own)
    edges = gconv.astype(BF16)
    gtop, gbot = shifted(edges, TALL, 0)
    gleft, gright = column_halo(edges, gtop, gbot)

    free = lambda n: [pl.BlockSpec(memory_space=pl.ANY)] * n
    joined = pl.pallas_call(
        join_kernel,
        out_shape=jax.ShapeDtypeStruct((PIECES, ROWS, LANES), BF16),
        in_specs=whole(2),
        out_specs=hbm(1)[0],
        scratch_shapes=[
            pltpu.VMEM((PIECES, ROWS, LANES), BF16),
            pltpu.SemaphoreType.DMA((PIECES,)),
        ],
        compiler_params=LIMIT,
        name="join",
    )(mine, got)
    near = lax.all_to_all(joined, ("zl", "xl", "yl"), 0, 0, tiled=True)
    by_block = pl.pallas_call(
        block_sum_kernel,
        out_shape=jax.ShapeDtypeStruct((FAR, FROWS, LANES), BF16),
        in_specs=smem + whole(1) + free(2),
        out_specs=whole(1)[0],
        scratch_shapes=[pltpu.VMEM((ROWS, LANES), F32)],
        compiler_params=LIMIT,
        name="block_sum",
    )(yl.reshape(1), near, gtop, gbot)
    grad_in = pl.pallas_call(
        input_grad_kernel,
        out_shape=jax.ShapeDtypeStruct((height, width, D), BF16),
        in_specs=whole(7),
        out_specs=whole(1)[0],
        scratch_shapes=[pltpu.VMEM((height + 2 * HALO, width + 8, D), F32)],
        compiler_params=LIMIT,
        name="input_grad",
    )(gconv, gtop, gbot, gleft, gright, cot_near, dwk_near)
    by_block = lax.all_to_all(by_block, ("zh", "xh", "yh"), 0, 0, tiled=True)
    grad_expand, grad_reduce_t, small = pl.pallas_call(
        functools.partial(far_sum_kernel, scale),
        out_shape=(
            jax.ShapeDtypeStruct((DROWS, FROWS), F32),
            jax.ShapeDtypeStruct((DROWS, FROWS), F32),
            jax.ShapeDtypeStruct((2 * PIECES, SHARE, LANES), F32),
        ),
        in_specs=whole(1) + free(2),
        out_specs=tuple(whole(3)),
        compiler_params=LIMIT,
        name="far_sum",
    )(by_block, gleft, gright)
    small = lax.all_to_all(small, ("zl", "xl", "yl", "core"), 0, 0, tiled=True)
    gker, vectors, gbexp = pl.pallas_call(
        spread_kernel,
        out_shape=(
            jax.ShapeDtypeStruct((7, 7, D), F32),
            jax.ShapeDtypeStruct((5, D), F32),
            jax.ShapeDtypeStruct((FF,), F32),
        ),
        in_specs=whole(1),
        out_specs=tuple(whole(3)),
        compiler_params=LIMIT,
        name="spread",
    )(small)
    return (
        block_out[None],
        grad_in[None],
        grad_expand,
        grad_reduce_t,
        gker,
        vectors,
        gbexp,
    )


def solution(mesh):
    shape = dict(mesh.shape)
    sizes = (shape["rows"] // 2, 2, shape["cols"] // 2, 2, shape["rep"] // 4, 2, 2)
    fine = Mesh(mesh.devices.reshape(sizes), TALL + WIDE + ("yh", "yl", "core"))
    tile = P(("yh", "yl", "core"), TALL, WIDE, None)
    grad = P(("yh", "yl", "core"), TALL + WIDE)
    pixels = 16 * 64 * 128
    scale = float(pixels) ** -0.5
    return jax.shard_map(
        functools.partial(per_device, scale),
        mesh=fine,
        in_specs=(tile,) + (P(),) * 9 + (tile,),
        out_specs=(tile, tile, grad, grad, P(), P(), P()),
        check_vma=False,
    )
```

```python
import functools

import jax
import jax.numpy as jnp
from jax import lax
from jax.experimental import pallas as pl
from jax.experimental.pallas import tpu as pltpu
from jax.sharding import Mesh
from jax.sharding import PartitionSpec as P

EPS = 1e-06
INV_ROOT_TWO = 0.7071067811865476
INV_ROOT_TWO_PI = 0.3989422804014327
F32 = jnp.float32
BF16 = jnp.bfloat16
D = 384
FF = 1536
LANES = 128
BLOCKS = D // LANES
HALO = 3
FROWS = 24
DROWS = 24
PIECES = 8
FAR = 64
BIG = BLOCKS * 8 * FROWS
SHARE = 12
ROWS = BIG + 2 * SHARE
TALL = ("zh", "zl")
WIDE = ("xh", "xl")
LIMIT = pltpu.CompilerParams(vmem_limit_bytes=30 * 1024 * 1024)


def matmul(a, b, ca, cb):
    return lax.dot_general(a, b, (((ca,), (cb,)), ((), ())), preferred_element_type=F32)


def fetch_kernel(*refs):
    count = len(refs) // 2
    copies = [
        pltpu.make_async_copy(refs[k], refs[count + k], refs[-1].at[k]) for k in range(count)
    ]
    for c in copies:
        c.start()
    for c in copies:
        c.wait()


def front_kernel(
    core_ref,
    x_ref,
    top_ref,
    bot_ref,
    left_ref,
    right_ref,
    cot_ref,
    dwk_ref,
    dwb_ref,
    gain_ref,
    lnb_ref,
    wexp_ref,
    bexp_ref,
    wred_ref,
    bred_ref,
    ls_ref,
    block_ref,
    gconv_ref,
    send_hbm,
    both,
    stack_ref,
    own_ref,
    xp,
    conv,
    small,
    send_ref,
    bias_ref,
    out_sems,
):
    first = pltpu.make_async_copy(dwb_ref, bias_ref, out_sems.at[6])
    first.start()
    height, width = x_ref.shape[0], x_ref.shape[1]
    pixels = height * width
    row = lambda ref: ref[...].reshape(1, -1)
    xp[0:HALO, HALO : HALO + width, :] = top_ref[...].astype(F32)
    xp[HALO + height :, HALO : HALO + width, :] = bot_ref[...].astype(F32)
    xp[:, 0:HALO, :] = left_ref[...].astype(F32)
    xp[:, HALO + width : 2 * HALO + width, :] = right_ref[...].astype(F32)
    small[...] = jnp.zeros_like(small)

    def put(p, l, value):
        at = BLOCKS * (p % 4) + l
        small[p // 4, at : at + 1, :] = value

    xp[HALO : HALO + height, HALO : HALO + width, :] = x_ref[...].astype(F32)
    for l in range(BLOCKS):
        ln = slice(LANES * l, LANES * (l + 1))
        acc = jnp.zeros((height, width, LANES), F32)
        for j in range(7):
            s = xp[:, j : j + width, ln]
            for i in range(7):
                acc = acc + dwk_ref[i, j : j + 1, ln] * s[i : i + height]
        conv[:, ln] = acc.reshape(pixels, LANES)
    first.wait()
    flat = conv[...] + row(bias_ref)
    centered = flat - jnp.mean(flat, axis=-1, keepdims=True)
    inv = lax.rsqrt(jnp.mean(centered * centered, axis=-1, keepdims=True) + EPS)
    xhat = centered * inv
    gain = row(gain_ref)
    normed = (xhat * gain + row(lnb_ref)).astype(BF16)
    grad = cot_ref[...].astype(F32).reshape(pixels, D)
    scaled = grad * row(ls_ref)
    g_branch = scaled.astype(BF16)
    for f in range(4):
        sl = slice(D * f, D * (f + 1))
        pre = matmul(normed, wexp_ref[:, sl], 1, 0) + bexp_ref[sl].reshape(1, D)
        cdf = 0.5 * (1.0 + lax.erf(pre * INV_ROOT_TWO))
        pdf = jnp.exp(-0.5 * pre * pre) * INV_ROOT_TWO_PI
        g_act = matmul(g_branch, wred_ref[sl, :], 1, 1)
        g_pre = g_act * (cdf + pre * pdf)
        both[0:pixels, sl] = g_pre.astype(BF16)
        both[pixels : 2 * pixels, sl] = (pre * cdf).astype(BF16)
        total = jnp.sum(g_pre, axis=0, keepdims=True)
        for l in range(BLOCKS):
            put(54 + f, l, total[:, LANES * l : LANES * (l + 1)])
    stack_ref[0:pixels, :] = normed
    stack_ref[pixels : 2 * pixels, :] = g_branch
    outputs = products(1 - core_ref[0], both, stack_ref[...], send_ref, send_hbm, out_sems)
    branch = matmul(both[pixels : 2 * pixels, :], wred_ref[...], 1, 0) + row(bred_ref)
    block = x_ref[...].astype(F32).reshape(pixels, D) + row(ls_ref) * branch
    block_ref[...] = block.astype(BF16).reshape(height, width, D)
    g_norm = matmul(both[0:pixels, :], wexp_ref[...], 1, 1)
    gx = g_norm * gain
    gconv = inv * (
        gx
        - jnp.mean(gx, axis=-1, keepdims=True)
        - xhat * jnp.mean(gx * xhat, axis=-1, keepdims=True)
    )
    gconv_ref[...] = gconv.reshape(height, width, D)
    sums = (gconv, g_norm * xhat, g_norm, scaled, grad * branch)
    for k, value in enumerate(sums):
        total = jnp.sum(value, axis=0, keepdims=True)
        for l in range(BLOCKS):
            put(49 + k, l, total[:, LANES * l : LANES * (l + 1)])
    for l in range(BLOCKS):
        ln = slice(LANES * l, LANES * (l + 1))
        g3 = gconv_ref[:, :, ln]
        for j in range(7):
            s = xp[:, j : j + width, ln]
            for i in range(7):
                part = jnp.sum(g3 * s[i : i + height], axis=0)
                put(7 * i + j, l, jnp.sum(part, axis=0, keepdims=True))
    value = small[:, 0:SHARE, :]
    small[:, SHARE : 2 * SHARE, :] = value - value.astype(BF16).astype(F32)
    core = core_ref[0]
    own_ref[...] = small[pl.ds(PIECES * core, PIECES)]
    send_ref[:, BIG:ROWS, :] = small[pl.ds(PIECES * (1 - core), PIECES)].astype(BF16)
    rows = slice(BIG, ROWS)
    c = pltpu.make_async_copy(send_ref.at[:, rows], send_hbm.at[:, rows], out_sems.at[6])
    c.start()
    for c in outputs + [c]:
        c.wait()


def products(core, both, stack, out, hbm, sems):
    pixels = stack.shape[0] // 2
    copies = []

    def flush(rows):
        c = pltpu.make_async_copy(out.at[:, rows], hbm.at[:, rows], sems.at[len(copies)])
        c.start()
        copies.append(c)

    chan = lax.broadcasted_iota(jnp.int32, (D, D), 0)
    column = lax.broadcasted_iota(jnp.int32, (1, D), 1)
    half = (column >= D // 2).astype(jnp.int32)
    rest = column - (D // 2) * half
    block = (rest * 1366) >> 16
    inside = rest - 2 * DROWS * block
    of_e = inside < DROWS
    base = 4 * DROWS * block + jnp.where(of_e, inside, inside - DROWS)
    pixel = lax.broadcasted_iota(jnp.int32, (2 * pixels, 1), 0)
    keep = jnp.where(pixel < pixels, 1, 0) == jnp.where(of_e, 1, 0)
    lane = lax.broadcasted_iota(jnp.int32, (1, 1, LANES), 2)
    right = []
    for order in range(2):
        turn = half if order == 0 else 1 - half
        pick = (chan == base + 2 * DROWS * turn + DROWS * core).astype(F32).astype(BF16)
        right.append(jnp.where(keep, matmul(stack, pick, 1, 0), 0.0).astype(BF16))
    for low in range(2):
        g = []
        for order in range(2):
            f = low + 2 * order
            part = matmul(both[:, D * f : D * (f + 1)], right[order], 0, 0)
            g.append(part.reshape(2, 4, 2, FROWS, D))
        for zl in range(2):
            for xl in range(2):
                for yl in range(2):
                    one, two = g[yl][zl, :, xl], g[1 - yl][zl, :, xl]
                    pieces = (
                        one[:, :, 0:LANES],
                        jnp.where(
                            lane < LANES // 2,
                            one[:, :, LANES : 2 * LANES],
                            two[:, :, LANES : 2 * LANES],
                        ),
                        two[:, :, 2 * LANES : D],
                    )
                    for l, piece in enumerate(pieces):
                        at = 8 * FROWS * l + 4 * FROWS * low
                        out[4 * zl + 2 * xl + yl, at : at + 4 * FROWS, :] = piece.reshape(
                            4 * FROWS, LANES
                        ).astype(BF16)
        for l in range(BLOCKS):
            at = 8 * FROWS * l + 4 * FROWS * low
            flush(slice(at, at + 4 * FROWS))
    return copies


def own_kernel(core_ref, both_ref, stack_ref, small_ref, out_hbm, out_ref, sems):
    out_ref[:, BIG:ROWS, :] = small_ref[...].astype(BF16)
    rows = slice(BIG, ROWS)
    c = pltpu.make_async_copy(out_ref.at[:, rows], out_hbm.at[:, rows], sems.at[6])
    c.start()
    for c in products(core_ref[0], both_ref, stack_ref[...], out_ref, out_hbm, sems) + [c]:
        c.wait()


def join_kernel(mine_ref, got_ref, out_hbm, out_ref, sems):
    both = mine_ref[:, BIG:ROWS, :].astype(F32) + got_ref[:, BIG:ROWS, :].astype(F32)
    value = both[:, 0:SHARE] + both[:, SHARE : 2 * SHARE]
    low = value - value.astype(BF16).astype(F32)
    out_ref[:, BIG:ROWS, :] = jnp.concatenate([value, low], axis=1).astype(BF16)
    copies = []
    for k in range(PIECES):
        big = mine_ref[k, 0:BIG, :].astype(F32) + got_ref[k, 0:BIG, :].astype(F32)
        out_ref[k, 0:BIG, :] = big.astype(BF16)
        c = pltpu.make_async_copy(out_ref.at[k], out_hbm.at[k], sems.at[k])
        c.start()
        copies.append(c)
    for c in copies:
        c.wait()


def block_sum_kernel(yl_ref, got_ref, top_any, bot_any, out_hbm, out_ref, total, sems):
    copies = []
    total[...] = jnp.sum(got_ref[...].astype(F32), axis=0)
    small = total[BIG : BIG + SHARE, :] + total[BIG + SHARE : ROWS, :]
    side = LANES // 2
    folded = jnp.concatenate([small[:, 0:side], small[:, side:]], axis=0)
    gap = jnp.zeros((FROWS, side - 2 * DROWS), F32)
    tail = jnp.concatenate([gap, folded], axis=1)
    for low in range(2):
        for xh in range(4):
            at = 4 * FROWS * low + FROWS * xh
            wide = jnp.concatenate(
                [
                    total[8 * FROWS * l + at : 8 * FROWS * l + at + FROWS, :]
                    for l in range(BLOCKS)
                ],
                axis=1,
            )
            for half in range(2):
                turn = yl_ref[0] if half == 0 else 1 - yl_ref[0]
                zh = low + 2 * turn
                for yh in range(4):
                    start = D // 2 * half + 2 * DROWS * yh
                    piece = jnp.concatenate([wide[:, start : start + 2 * DROWS], tail], axis=1)
                    out_ref[16 * zh + 4 * xh + yh] = piece.astype(BF16)
        for k, zh in enumerate((low, low + 2)):
            at = slice(16 * zh, 16 * (zh + 1))
            c = pltpu.make_async_copy(out_ref.at[at], out_hbm.at[at], sems.at[2 * low + k])
            c.start()
            copies.append(c)
    for c in copies:
        c.wait()


def far_sum_kernel(scale, got_ref, left_any, right_any, ge_ref, gr_ref, small_ref):
    total = jnp.sum(got_ref[...].astype(F32), axis=0) * scale
    turned = jnp.transpose(total, (1, 0))
    ge_ref[...] = turned[0:DROWS, 0:FROWS]
    gr_ref[...] = turned[DROWS : 2 * DROWS, 0:FROWS]
    side = LANES // 2
    small = jnp.concatenate([total[0:SHARE, side:], total[SHARE:FROWS, side:]], axis=1)
    small_ref[...] = jnp.broadcast_to(small, small_ref.shape)


def spread_kernel(got_ref, gker_ref, vec_ref, gbexp_ref):
    def take(p, l):
        share, at = p // 4, BLOCKS * (p % 4) + l
        return got_ref[2 * (share % PIECES) + share // PIECES, at : at + 1, :]

    for l in range(BLOCKS):
        ln = slice(LANES * l, LANES * (l + 1))
        for i in range(7):
            for j in range(7):
                gker_ref[i, j : j + 1, ln] = take(7 * i + j, l)
        for k in range(5):
            vec_ref[k : k + 1, ln] = take(49 + k, l)
        for f in range(4):
            at = D * f + LANES * l
            gbexp_ref[at : at + LANES] = take(54 + f, l).reshape(LANES)


def input_grad_kernel(g_ref, top_ref, bot_ref, left_ref, right_ref, cot_ref, dwk_ref, out_ref, gp):
    height, width = g_ref.shape[0], g_ref.shape[1]
    gp[HALO : HALO + height, HALO : HALO + width, :] = g_ref[...]
    gp[0:HALO, HALO : HALO + width, :] = top_ref[...].astype(F32)
    gp[HALO + height :, HALO : HALO + width, :] = bot_ref[...].astype(F32)
    gp[:, 0:HALO, :] = left_ref[...].astype(F32)
    gp[:, HALO + width : 2 * HALO + width, :] = right_ref[...].astype(F32)
    for l in range(BLOCKS):
        ln = slice(LANES * l, LANES * (l + 1))
        acc = cot_ref[:, :, ln].astype(F32)
        for j in range(7):
            s = gp[:, 6 - j : 6 - j + width, ln]
            for i in range(7):
                acc = acc + dwk_ref[i, j : j + 1, ln] * s[6 - i : 6 - i + height]
        out_ref[:, :, ln] = acc.astype(BF16)


def shifted(cells, axis, dim):
    count = lax.axis_size(axis)
    size = cells.shape[dim]
    head = lax.slice_in_dim(cells, 0, HALO, axis=dim)
    tail = lax.slice_in_dim(cells, size - HALO, size, axis=dim)
    before = lax.ppermute(tail, axis, [(i, i + 1) for i in range(count - 1)])
    after = lax.ppermute(head, axis, [(i + 1, i) for i in range(count - 1)])
    return before, after


def column_halo(cells, top, bot):
    width = cells.shape[1]
    head = jnp.concatenate([a[:, 0:HALO] for a in (top, cells, bot)], axis=0)
    tail = jnp.concatenate([a[:, width - HALO :] for a in (top, cells, bot)], axis=0)
    count = lax.axis_size(WIDE)
    left = lax.ppermute(tail, WIDE, [(i, i + 1) for i in range(count - 1)])
    right = lax.ppermute(head, WIDE, [(i + 1, i) for i in range(count - 1)])
    return left, right


def per_device(
    scale,
    feature_map,
    dw_kernel,
    dw_bias,
    layer_norm_gain,
    layer_norm_bias,
    w_expand,
    b_expand,
    w_reduce,
    b_reduce,
    layer_scale,
    cotangent,
):
    x, cot = feature_map[0], cotangent[0]
    height, width = x.shape[0], x.shape[1]
    core = lax.axis_index("core").astype(jnp.int32)
    yl = lax.axis_index("yl").astype(jnp.int32)
    top, bot = shifted(x, TALL, 0)

    whole = lambda n: [pl.BlockSpec(memory_space=pltpu.VMEM)] * n
    away = lambda v: pltpu.with_memory_space_constraint(v, pltpu.HBM)
    hbm = lambda n: [pl.BlockSpec(memory_space=pltpu.HBM)] * n
    fetched = (
        x,
        cot,
        dw_kernel,
        w_expand,
        w_reduce,
        dw_bias,
        layer_norm_gain,
        layer_norm_bias,
        b_expand,
        b_reduce,
        layer_scale,
    )
    x_near, cot_near, dwk_near, wexp_near, wred_near, dwb, gain, lnb, bexp, bred, ls = pl.pallas_call(
        fetch_kernel,
        out_shape=tuple(jax.ShapeDtypeStruct(v.shape, v.dtype) for v in fetched),
        in_specs=hbm(11),
        out_specs=tuple(whole(11)),
        scratch_shapes=[pltpu.SemaphoreType.DMA((11,))],
        compiler_params=LIMIT,
        name="fetch",
    )(*[away(v) for v in fetched])
    left, right = column_halo(x_near, top, bot)
    smem = [pl.BlockSpec(memory_space=pltpu.SMEM)]
    pixels = height * width
    block_out, gconv, send, both, stack, own = pl.pallas_call(
        front_kernel,
        out_shape=(
            jax.ShapeDtypeStruct((height, width, D), BF16),
            jax.ShapeDtypeStruct((height, width, D), F32),
            jax.ShapeDtypeStruct((PIECES, ROWS, LANES), BF16),
            jax.ShapeDtypeStruct((2 * pixels, FF), BF16),
            jax.ShapeDtypeStruct((2 * pixels, D), BF16),
            jax.ShapeDtypeStruct((PIECES, 2 * SHARE, LANES), F32),
        ),
        in_specs=smem + whole(15),
        out_specs=tuple(whole(2) + hbm(1) + whole(3)),
        scratch_shapes=[
            pltpu.VMEM((height + 2 * HALO, width + 8, D), F32),
            pltpu.VMEM((pixels, D), F32),
            pltpu.VMEM((2 * PIECES, 2 * SHARE, LANES), F32),
            pltpu.VMEM((PIECES, ROWS, LANES), BF16),
            pltpu.VMEM((D,), F32),
            pltpu.SemaphoreType.DMA((7,)),
        ],
        compiler_params=LIMIT,
        name="front",
    )(
        core.reshape(1),
        x_near,
        top,
        bot,
        left,
        right,
        cot_near,
        dwk_near,
        dwb,
        gain,
        lnb,
        wexp_near,
        bexp,
        wred_near,
        bred,
        ls,
    )

    got = lax.ppermute(send, "core", [(0, 1), (1, 0)])
    mine = pl.pallas_call(
        own_kernel,
        out_shape=jax.ShapeDtypeStruct((PIECES, ROWS, LANES), BF16),
        in_specs=smem + whole(3),
        out_specs=hbm(1)[0],
        scratch_shapes=[
            pltpu.VMEM((PIECES, ROWS, LANES), BF16),
            pltpu.SemaphoreType.DMA((7,)),
        ],
        compiler_params=LIMIT,
        name="own",
    )(core.reshape(1), both, stack, own)
    edges = gconv.astype(BF16)
    gtop, gbot = shifted(edges, TALL, 0)
    gleft, gright = column_halo(edges, gtop, gbot)

    free = lambda n: [pl.BlockSpec(memory_space=pl.ANY)] * n
    joined = pl.pallas_call(
        join_kernel,
        out_shape=jax.ShapeDtypeStruct((PIECES, ROWS, LANES), BF16),
        in_specs=whole(2),
        out_specs=hbm(1)[0],
        scratch_shapes=[
            pltpu.VMEM((PIECES, ROWS, LANES), BF16),
            pltpu.SemaphoreType.DMA((PIECES,)),
        ],
        compiler_params=LIMIT,
        name="join",
    )(mine, got)
    near = lax.all_to_all(joined, ("zl", "xl", "yl"), 0, 0, tiled=True)
    by_block = pl.pallas_call(
        block_sum_kernel,
        out_shape=jax.ShapeDtypeStruct((FAR, FROWS, LANES), BF16),
        in_specs=smem + whole(1) + free(2),
        out_specs=hbm(1)[0],
        scratch_shapes=[
            pltpu.VMEM((FAR, FROWS, LANES), BF16),
            pltpu.VMEM((ROWS, LANES), F32),
            pltpu.SemaphoreType.DMA((4,)),
        ],
        compiler_params=LIMIT,
        name="block_sum",
    )(yl.reshape(1), near, gtop, gbot)
    grad_in = pl.pallas_call(
        input_grad_kernel,
        out_shape=jax.ShapeDtypeStruct((height, width, D), BF16),
        in_specs=whole(7),
        out_specs=whole(1)[0],
        scratch_shapes=[pltpu.VMEM((height + 2 * HALO, width + 8, D), F32)],
        compiler_params=LIMIT,
        name="input_grad",
    )(gconv, gtop, gbot, gleft, gright, cot_near, dwk_near)
    by_block = lax.all_to_all(by_block, ("zh", "xh", "yh"), 0, 0, tiled=True)
    grad_expand, grad_reduce_t, small = pl.pallas_call(
        functools.partial(far_sum_kernel, scale),
        out_shape=(
            jax.ShapeDtypeStruct((DROWS, FROWS), F32),
            jax.ShapeDtypeStruct((DROWS, FROWS), F32),
            jax.ShapeDtypeStruct((2 * PIECES, SHARE, LANES), F32),
        ),
        in_specs=whole(1) + free(2),
        out_specs=tuple(whole(3)),
        compiler_params=LIMIT,
        name="far_sum",
    )(by_block, gleft, gright)
    small = lax.all_to_all(small, ("zl", "xl", "yl", "core"), 0, 0, tiled=True)
    gker, vectors, gbexp = pl.pallas_call(
        spread_kernel,
        out_shape=(
            jax.ShapeDtypeStruct((7, 7, D), F32),
            jax.ShapeDtypeStruct((5, D), F32),
            jax.ShapeDtypeStruct((FF,), F32),
        ),
        in_specs=whole(1),
        out_specs=tuple(whole(3)),
        compiler_params=LIMIT,
        name="spread",
    )(small)
    return (
        block_out[None],
        grad_in[None],
        grad_expand,
        grad_reduce_t,
        gker,
        vectors,
        gbexp,
    )


def solution(mesh):
    shape = dict(mesh.shape)
    sizes = (shape["rows"] // 2, 2, shape["cols"] // 2, 2, shape["rep"] // 4, 2, 2)
    fine = Mesh(mesh.devices.reshape(sizes), TALL + WIDE + ("yh", "yl", "core"))
    tile = P(("yh", "yl", "core"), TALL, WIDE, None)
    grad = P(("yh", "yl", "core"), TALL + WIDE)
    pixels = 16 * 64 * 128
    scale = float(pixels) ** -0.5
    return jax.shard_map(
        functools.partial(per_device, scale),
        mesh=fine,
        in_specs=(tile,) + (P(),) * 9 + (tile,),
        out_specs=(tile, tile, grad, grad, P(), P(), P()),
        check_vma=False,
    )
```
